32 devices in a mesh: groups: 2 (over y), row: 16 (over z, x, core).
Axes of the slice: x: 2, y: 2, z: 4, core: 2. Of those that a mesh axis runs over, the one named last changes fastest.
Arguments:
- activations: bfloat16 [768, 8192], P('groups', 'row'), parts along dimension 0, may hold values from -24 to 24
- norm_gain: bfloat16 [8192], P('row'), may hold values from 0.099609375 to 1.8984375
- gate_weight: bfloat16 [8192, 28672], P(None, 'row'), may hold values from -0.0625 to 0.0625
- up_weight: bfloat16 [8192, 28672], P(None, 'row'), may hold values from -0.0625 to 0.0625
- down_weight: bfloat16 [28672, 8192], P('row'), may hold values from -0.046875 to 0.046875
Outputs:
- mlp_out: bfloat16 [768, 8192], P('groups', 'row'), parts along dimension 0
The draws below stay inside these ranges and needn't reach their ends.
There are 2 independent parts, one for each index of `groups`. The reference program is written for one: setup_inputs(seed, part) draws one part's arguments, and reference() takes and returns one part's arrays. A program takes and returns all parts, laid end to end along the dimension named above; an argument that names none is the same for every part. Nothing has to cross between parts.
All inputs are finite; a program needn't handle non-finite values.
Results may differ from the reference program's by a relative error of at most 0.0065.
Values may be sent and summed in bfloat16 or wider, within the bound.
A program may use at most 192 MiB of HBM per device.

```python
import jax
import jax.numpy as jnp
from jax import lax

D = 8192
FF = 28672
TOKENS = 384


def draw_activations(key, part):
    key_cols, key_rows, key_base = jax.random.split(key, 3)
    position = jnp.arange(D, dtype=jnp.float32) / max(D - 1, 1)
    column_scale = jnp.exp(jax.random.uniform(key_cols, (D,), jnp.float32) * jnp.log(10.0))
    row_scale = jnp.exp(jax.random.uniform(key_rows, (TOKENS, 1), jnp.float32) * jnp.log(10.0))
    rising = 3.0 ** position
    base_values = jax.random.truncated_normal(key_base, -4.0, 4.0, (TOKENS, D), jnp.float32)
    result = jnp.clip(base_values * row_scale * (column_scale * rising)[None, :] * 0.05, -24.0, 24.0)
    return result.astype(jnp.bfloat16)


def strengthened(values, rng, source, target, shards_of, factor):
    owner, partner = [(jnp.arange(values.shape[dim]) // (values.shape[dim] // shards_of)).reshape([-1 if axis == dim else 1 for axis in range(values.ndim)]) for dim in (source, target)]
    chosen = jax.random.permutation(rng, shards_of)[partner]
    strong = (owner == chosen) | (owner == (partner + shards_of // 2) % shards_of)
    return jnp.where(strong, factor * values, values)


def block_scale(rng, shape, pieces, low, top_value):
    def one(dim, parts):
        heights = jax.random.uniform(jax.random.fold_in(jax.random.fold_in(rng, 6), dim), (parts,), jnp.float32, low / len(pieces), top_value / len(pieces))
        return jnp.repeat(jnp.exp(heights), shape[dim] // parts).reshape((-1,) + (1,) * (len(shape) - dim - 1))

    gain = one(*pieces[0])
    for cut in pieces[1:]:
        gain = gain * one(*cut)
    return gain


def bell_draw(key, extent, spread, limit, shards=(), kind=jnp.bfloat16):
    values = jax.random.normal(key, extent, jnp.float32) * spread
    if len(shards) > 0:
        values = block_scale(key, extent, shards, -0.22, 0.18) * values
    return jnp.clip(values, min=-limit, max=limit).astype(kind)


def gaussian_with(own_key, extent, scale, reach, cuts, heavy, held_as=jnp.bfloat16):
    values = scale * jax.random.normal(own_key, extent, jnp.float32)
    if cuts:
        values = values * block_scale(own_key, extent, cuts, -0.22, 0.18)
    return jnp.clip(strengthened(values, jax.random.fold_in(own_key, 3), *heavy), -reach, reach).astype(held_as)


def setup_inputs(seed: int = 0, part: int = 0) -> dict:
    arg_keys = jax.random.split(jax.random.key(seed), 6)
    own_keys = jax.random.split(jax.random.fold_in(arg_keys[5], part), 6)
    activations = draw_activations(jax.random.fold_in(jax.random.fold_in(arg_keys[5], part), 71), part)
    norm_gain = jnp.clip(1.0 + 0.18 * jax.random.normal(arg_keys[1], (D,), jnp.float32), 0.099609375, 1.8984375).astype(jnp.bfloat16)
    gate_weight = bell_draw(arg_keys[2], (D, FF), D ** -0.5, 0.0625, ((1, 16),))
    up_weight = bell_draw(arg_keys[3], (D, FF), D ** -0.5, 0.0625, ((1, 16),))
    down_weight = gaussian_with(arg_keys[4], (FF, D), FF ** -0.5, 0.046875, ((0, 16),), (0, 1, 16, 2.0))
    return {"activations": activations, "norm_gain": norm_gain, "gate_weight": gate_weight, "up_weight": up_weight, "down_weight": down_weight}


def reference(activations, norm_gain, gate_weight, up_weight, down_weight):
    float_rows = activations.astype(jnp.float32)
    mean_square = lax.optimization_barrier(jnp.mean(float_rows * float_rows, axis=1, keepdims=True))
    normed = (float_rows * lax.rsqrt(mean_square + 1e-05) * norm_gain.astype(jnp.float32)[None, :]).astype(jnp.bfloat16)
    gate_proj = jnp.dot(normed, gate_weight, preferred_element_type=jnp.float32)
    up_proj = jnp.dot(normed, up_weight, preferred_element_type=jnp.float32)
    hidden = (jax.nn.silu(gate_proj) * up_proj).astype(jnp.bfloat16)
    return jnp.dot(hidden, down_weight, preferred_element_type=jnp.float32).astype(jnp.bfloat16)
```

```python
import jax
import jax.numpy as jnp
from jax import lax
from jax.experimental import pallas as pl
from jax.experimental.pallas import tpu as pltpu
from jax.sharding import PartitionSpec as P

D = 8192
Z, X, H = 4, 2, 2
STEPS = Z * X * H
SLOTS = 4
MESH = pl.DeviceIdType.MESH


GATHER_END = (0, 1, 4, 2, 5, 3, 8, 6, 9, 7, 12, 10, 13, 11, 14, 15)
GATHER_MID = (4, 5, 8, 0, 6, 9, 1, 7, 12, 2, 13, 3, 10, 11, 15, 14)
LATE, LATE_AT = 12, 11
INNER_END, INNER_MID, OUTER_MID = 5, 7, 14
REDUCE_END = (14, 15, 10, 13, 11, 6, 12, 7, 2, 8, 3, 9, 4, 5, 0, 1)
REDUCE_MID = (14, 3, 11, 2, 15, 10, 6, 7, 13, 12, 1, 8, 0, 9, 4, 5)


def plain(activations, norm_gain, gate_weight, up_weight, down_weight):
    float_rows = activations.astype(jnp.float32)
    square_sums = lax.psum(jnp.sum(float_rows * float_rows, axis=1), "row")
    inv_scale = lax.rsqrt(square_sums / D + 1e-05)
    normed = (float_rows * inv_scale[:, None] * norm_gain.astype(jnp.float32)[None, :]).astype(
        jnp.bfloat16
    )
    shard_rows = lax.all_gather(normed, "row", axis=1, tiled=True)
    gate_proj = jnp.dot(shard_rows, gate_weight, preferred_element_type=jnp.float32)
    up_proj = jnp.dot(shard_rows, up_weight, preferred_element_type=jnp.float32)
    hidden = (jax.nn.silu(gate_proj) * up_proj).astype(jnp.bfloat16)
    reduced = lax.psum_scatter(
        lax.dot_general(
            down_weight, hidden, (((0,), (1,)), ((), ())), preferred_element_type=jnp.float32
        ),
        "row",
        scatter_dimension=0,
        tiled=True,
    )
    return reduced.T.astype(jnp.bfloat16)


def kernel(
    act, gain, gate_w, up_w, down_w, out,
    act_buf, gathered, stats, squares, inv, w_buf, acc, hidden, dw_buf,
    core_out, core_in, x_out, x_in, z_out, z_in, e_out, e_in, total, result,
    act_sem, out_sem, w_sem, dw_sem, s_recv, s_core, s_x, s_up, s_down,
    g_recv, g_up, g_down, g_x, g_core, g_extra,
    core_send, core_recv, x_send, x_recv, z_send, z_recv, e_send, e_recv,
):
    n = 2 * Z * X
    bf16, f32 = jnp.bfloat16, jnp.float32
    me = lax.axis_index("row")
    c = lax.rem(me, 2)
    x = lax.rem(me // 2, X)
    z = me // (2 * X)
    tokens, wide = hidden.shape
    feat = act_buf.shape[1]
    half = feat // H
    end = (z == 0) | (z == Z - 1)
    mid = jnp.logical_not(end)
    low = z < Z // 2
    partner = me + 1 - 2 * c
    across = me + 2 - 4 * x
    above = jnp.minimum(me + 2 * X, n - 1)
    below = jnp.maximum(me - 2 * X, 0)
    inner = jnp.where(low, above, below)
    outer = jnp.where(low, below, above)
    my_cols = pl.ds(pl.multiple_of(c * half, half), half)

    def remote(src, dst, send, recv, target):
        return pltpu.make_async_remote_copy(
            src_ref=src, dst_ref=dst, send_sem=send, recv_sem=recv,
            device_id={"row": target}, device_id_type=MESH,
        )

    def pick(table, index):
        value = jnp.int32(table[0])
        for at in range(1, len(table)):
            value = jnp.where(index == at, jnp.int32(table[at]), value)
        return value

    def gather_code(s):
        return jnp.where(end, pick(GATHER_END, s), pick(GATHER_MID, s))

    def reduce_code(i):
        return jnp.where(end, pick(REDUCE_END, i), pick(REDUCE_MID, i))

    def by_z(plane, h):
        return (h == 1) & jnp.where(end, plane == Z - 1, (plane == 0) | (plane == 2))

    def decode(code):
        plane = code // 4
        p = jnp.where(low, plane, Z - 1 - plane)
        other = lax.rem(code // 2, 2)
        h = lax.rem(code, 2)
        chip = p * X + jnp.where(other == 1, 1 - x, x)
        return other == 0, h, plane, p, chip

    def weights(s):
        _, h, _, _, chip = decode(gather_code(s))
        slot = lax.rem(s, SLOTS)
        copies = []
        for i, w in enumerate((gate_w, up_w)):
            for core in range(2):
                start = (chip * 2 + core) * feat + h * half
                rows = pl.ds(pl.multiple_of(start, half), half)
                copies.append(
                    pltpu.make_async_copy(
                        w.at[rows],
                        w_buf.at[slot, i, pl.ds(core * half, half)],
                        w_sem.at[slot, i, core],
                    )
                )
        return copies

    def down(i):
        _, h, _, _, chip = decode(reduce_code(i))
        slot = lax.rem(i, SLOTS)
        copies = []
        for mine in range(2):
            core = c if mine else 1 - c
            start = (chip * 2 + core) * feat + h * half
            cols = pl.ds(pl.multiple_of(start, half), half)
            copies.append(
                pltpu.make_async_copy(
                    down_w.at[:, cols],
                    dw_buf.at[slot, :, pl.ds(mine * half, half)],
                    dw_sem.at[slot, mine],
                )
            )
        return copies

    own = pltpu.make_async_copy(act, act_buf, act_sem)
    own.start()
    for copy in weights(jnp.int32(0)):
        copy.start()

    barrier = pltpu.get_barrier_semaphore()

    def greet(target):
        pl.semaphore_signal(barrier, inc=1, device_id={"row": target}, device_id_type=MESH)

    greet(partner)
    greet(across)

    @pl.when(z < Z - 1)
    def _():
        greet(above)

    @pl.when(z > 0)
    def _():
        greet(below)

    blocks = tokens // 128
    mine_at = (z * X + x) * H
    gains = gain[...].astype(f32)
    with jax.named_scope("own_wait"):
        own.wait()
    for s in range(1, SLOTS):
        for copy in weights(jnp.int32(s)):
            copy.start()
    for h in range(H):
        for j in range(half // 128):
            at = h * (half // 128) + j
            part = act_buf[:, at * 128 : (at + 1) * 128].astype(f32) * gains[at : at + 1, :]
            cols = pl.ds(pl.multiple_of(c * half + j * 128, 128), 128)
            gathered[mine_at + h, :, cols] = part.astype(bf16)
    with jax.named_scope("barrier_wait"):
        pl.semaphore_wait(barrier, jnp.where(end, 3, 4))

    def pass_core(at):
        ref = gathered.at[at, :, my_cols]
        return remote(ref, ref, g_core.at[at], g_recv.at[at, c], partner)

    def passed(p, chip, h, send, target):
        ref, recv = gathered.at[chip * H + h, :, my_cols], g_recv.at[chip * H + h, c]
        return remote(ref, ref, send.at[p * H + h], recv, target)

    def pass_x(p, chip, h):
        return passed(p, chip, h, g_x, across)

    def pass_up(p, chip, h):
        return passed(p, chip, h, g_up, above)

    def pass_down(p, chip, h):
        return passed(p, chip, h, g_down, below)

    def tell(chip, send, target):
        ref = stats.at[chip * 2 + c]
        return remote(ref, ref, send, s_recv.at[chip * 2 + c], target)

    def told(chip, core):
        ref = stats.at[chip * 2 + core]
        pltpu.make_async_copy(ref, ref, s_recv.at[chip * 2 + core]).wait()

    def tell_on(in_line, p, chip):
        tell(chip, s_core.at[chip], partner).start()

        @pl.when(in_line)
        def _():
            tell(chip, s_x.at[p], across).start()

        @pl.when(in_line & (p <= z) & (z < Z - 1))
        def _():
            tell(chip, s_up.at[p], above).start()

        @pl.when(in_line & (p >= z) & (z > 0))
        def _():
            tell(chip, s_down.at[p], below).start()

    def extra(to_inner):
        plane = jnp.where(end, 0, 1) if to_inner else jnp.int32(Z - 1)
        p = jnp.where(low, plane, Z - 1 - plane)
        at = (p * X + 1 - x) * H + 1
        ref, recv = gathered.at[at, :, my_cols], g_recv.at[at, c]
        return remote(ref, ref, g_extra.at[to_inner], recv, inner if to_inner else outer)

    def arrived(s, core):
        _, h, _, _, chip = decode(gather_code(s))
        at = chip * H + h
        cols = pl.ds(pl.multiple_of(core * half, half), half)
        ref = gathered.at[at, :, cols]
        pltpu.make_async_copy(ref, ref, g_recv.at[at, core]).wait()

    def forward(s):
        in_line, h, plane, p, chip = decode(gather_code(s))
        pass_core(chip * H + h).start()
        late = mid & (gather_code(s) == LATE)

        @pl.when(in_line & jnp.logical_not(by_z(plane, h) | late))
        def _():
            pass_x(p, chip, h).start()

        @pl.when(in_line & (p <= z) & (z < Z - 1))
        def _():
            pass_up(p, chip, h).start()

        @pl.when(in_line & (p >= z) & (z > 0))
        def _():
            pass_down(p, chip, h).start()

        @pl.when(mid & (s == LATE_AT))
        def _():
            _, late_h, _, late_p, late_chip = decode(jnp.int32(LATE))
            pass_x(late_p, late_chip, late_h).start()

        @pl.when((h == 1) & (s >= H))
        def _():
            told(chip, c)
            tell_on(in_line, p, chip)

        @pl.when(s == jnp.where(end, INNER_END, INNER_MID))
        def _():
            extra(1).start()

        @pl.when(mid & (s == OUTER_MID))
        def _():
            extra(0).start()

    for h in range(H):
        forward(jnp.int32(h))

    rows = act_buf[...].astype(f32)
    sums = jnp.sum(rows * rows, axis=1, keepdims=True)
    squares[...] = jnp.broadcast_to(sums, (tokens, 128))
    for b in range(blocks):
        stats[me, b : b + 1, :] = squares[b * 128 : (b + 1) * 128, :].T[0:1, :]

    tell_on(True, z, z * X + x)
    acc[...] = jnp.zeros_like(acc)

    def gather_step(s, carry):
        _, h, _, _, chip = decode(gather_code(s))
        slot = lax.rem(s, SLOTS)
        at = chip * H + h
        even = lax.rem(s, 2) == 0

        @pl.when((s >= H - 1) & (s < STEPS - 1) & (mid | jnp.logical_not(even)))
        def _():
            with jax.named_scope("link_wait0"):
                arrived(s + 1, c)
            forward(s + 1)

        @pl.when(end & (s >= H - 1) & (s < STEPS - 1) & jnp.logical_not(even))
        def _():
            with jax.named_scope("link_wait1"):
                arrived(s + 2, c)
            forward(s + 2)

        with jax.named_scope("weight_wait"):
            for copy in weights(s):
                copy.wait()
        with jax.named_scope("partner_wait"):
            arrived(s, 1 - c)
        for i in range(2):
            acc[i] += jnp.dot(gathered[at], w_buf[slot, i], preferred_element_type=f32)

        @pl.when(s < STEPS - SLOTS)
        def _():
            for copy in weights(s + SLOTS):
                copy.start()

        @pl.when((s >= STEPS // 2) & (s < STEPS // 2 + SLOTS))
        def _():
            for copy in down(s - STEPS // 2):
                copy.start()

        return carry

    with jax.named_scope("gather"):
        lax.fori_loop(0, STEPS, gather_step, 0)

    for chip in range(Z * X):
        told(chip, 1 - c)
    sums = stats[0]
    for origin in range(1, n):
        sums = sums + stats[origin]
    scale = lax.rsqrt(sums / (n * feat) + 1e-05)
    for b in range(blocks):
        inv[b * 128 : (b + 1) * 128, :] = jnp.broadcast_to(scale[b : b + 1, :], (128, 128)).T

    def activate(t, carry):
        cols = pl.ds(pl.multiple_of(t * 128, 128), 128)
        by_two = 0.5 * (acc[0, :, cols] * inv[...])
        up = acc[1, :, cols] * inv[...]
        hidden[:, cols] = (by_two * (1.0 + jnp.tanh(by_two)) * up).astype(bf16)
        return carry

    with jax.named_scope("activation"):
        lax.fori_loop(0, wide // 128, activate, 0)

    def core_copy(i):
        return remote(core_out.at[i], core_in.at[i], core_send.at[i], core_recv.at[i], partner)

    def x_copy(at):
        return remote(x_out.at[at], x_in.at[at], x_send.at[at], x_recv.at[at], across)

    def z_copy(at, side, target):
        return remote(z_out.at[at], z_in.at[side, at], z_send.at[at], z_recv.at[side, at], target)

    def e_copy(side, target):
        return remote(e_out.at[side], e_in.at[side], e_send.at[side], e_recv.at[side], target)

    def out_copy(h):
        cols = pl.ds(pl.multiple_of(h * half, half), half)
        return pltpu.make_async_copy(result.at[h], out.at[:, cols], out_sem.at[h])

    def finish(j):
        in_line, h, plane, p, chip = decode(reduce_code(j))
        cross = jnp.logical_not(in_line)
        special = by_z(plane, h)
        at = p * H + h
        slot = lax.rem(j, 2)
        from_inner = cross & (h == 1) & (p == z)
        from_outer = cross & (h == 1) & mid & (plane == Z - 1)
        with jax.named_scope("core_wait"):
            core_copy(j).wait_recv()
        total[slot] += core_in[j].astype(f32)

        @pl.when(in_line & jnp.logical_not(special))
        def _():
            with jax.named_scope("x_wait"):
                x_copy(at).wait_recv()
            total[slot] += x_in[at].astype(f32)

        @pl.when(in_line & (z > 0) & (p >= z))
        def _():
            with jax.named_scope("zb_wait"):
                z_copy(at, 0, above).wait_recv()
            total[slot] += z_in[0, at].astype(f32)

        @pl.when(in_line & (z < Z - 1) & (p <= z))
        def _():
            with jax.named_scope("za_wait"):
                z_copy(at, 1, below).wait_recv()
            total[slot] += z_in[1, at].astype(f32)

        @pl.when(jnp.where(low, from_outer, from_inner))
        def _():
            with jax.named_scope("e_wait"):
                e_copy(0, above).wait_recv()
            total[slot] += e_in[0].astype(f32)

        @pl.when(jnp.where(low, from_inner, from_outer))
        def _():
            with jax.named_scope("e_wait"):
                e_copy(1, below).wait_recv()
            total[slot] += e_in[1].astype(f32)

        @pl.when(in_line & (p == z))
        def _():
            result[h] = total[slot].astype(bf16)
            out_copy(h).start()

        @pl.when(in_line & (p != z))
        def _():
            z_out[at] = total[slot].astype(bf16)

        @pl.when(in_line & (p > z))
        def _():
            z_copy(at, 0, above).start()

        @pl.when(in_line & (p < z))
        def _():
            z_copy(at, 1, below).start()

        @pl.when(cross & jnp.logical_not(special))
        def _():
            x_out[at] = total[slot].astype(bf16)
            x_copy(at).start()

        @pl.when(cross & special & (p > z))
        def _():
            e_out[0] = total[slot].astype(bf16)
            e_copy(0, above).start()

        @pl.when(cross & special & (p < z))
        def _():
            e_out[1] = total[slot].astype(bf16)
            e_copy(1, below).start()

    def reduce_step(i, carry):
        @pl.when(i < STEPS)
        def _():
            slot = lax.rem(i, SLOTS)
            for copy in down(i):
                copy.wait()
            part = jnp.dot(hidden[...], dw_buf[slot], preferred_element_type=f32)
            core_out[i] = part[:, :half].astype(bf16)
            core_copy(i).start()
            total[lax.rem(i, 2)] = part[:, half:]

        @pl.when(i < STEPS - SLOTS)
        def _():
            for copy in down(i + SLOTS):
                copy.start()

        @pl.when(i > 0)
        def _():
            with jax.named_scope("finish"):
                finish(i - 1)

        return carry

    with jax.named_scope("reduce"):
        lax.fori_loop(0, STEPS + 1, reduce_step, 0)

    for chip in range(Z * X):
        tell(chip, s_core.at[chip], partner).wait_send()
    for s in range(STEPS):
        pass_core(s).wait_send()
        core_copy(s).wait_send()
    extra(1).wait_send()
    for p in range(Z):
        plane = jnp.where(low, p, Z - 1 - p)
        for h in range(H):
            crosses = jnp.logical_not(by_z(plane, h))

            @pl.when(crosses)
            def _():
                pass_x(p, p * X, h).wait_send()
                x_copy(p * H + h).wait_send()

            @pl.when((p <= z) & (z < Z - 1))
            def _():
                pass_up(p, p * X, h).wait_send()

            @pl.when((p >= z) & (z > 0))
            def _():
                pass_down(p, p * X, h).wait_send()

            @pl.when(p != z)
            def _():
                z_copy(p * H + h, 0, above).wait_send()

        tell(p * X, s_x.at[p], across).wait_send()

        @pl.when((p <= z) & (z < Z - 1))
        def _():
            tell(p * X, s_up.at[p], above).wait_send()

        @pl.when((p >= z) & (z > 0))
        def _():
            tell(p * X, s_down.at[p], below).wait_send()

    @pl.when(mid)
    def _():
        extra(0).wait_send()

    @pl.when(mid | low)
    def _():
        e_copy(0, above).wait_send()

    @pl.when(mid | jnp.logical_not(low))
    def _():
        e_copy(1, below).wait_send()

    for h in range(H):
        out_copy(h).wait()


def fused(activations, norm_gain, gate_weight, up_weight, down_weight):
    tokens, feat = activations.shape
    wide = gate_weight.shape[1]
    n, half = 2 * Z * X, feat // H
    bf16, f32 = jnp.bfloat16, jnp.float32
    anywhere = pl.BlockSpec(memory_space=pl.ANY)
    vmem = pl.BlockSpec(memory_space=pltpu.VMEM)
    dma = pltpu.SemaphoreType.DMA
    return pl.pallas_call(
        kernel,
        out_shape=jax.ShapeDtypeStruct((tokens, feat), bf16),
        in_specs=[anywhere, vmem, anywhere, anywhere, anywhere],
        out_specs=anywhere,
        scratch_shapes=[
            pltpu.VMEM((tokens, feat), bf16),
            pltpu.VMEM((STEPS, tokens, 2 * half), bf16),
            pltpu.VMEM((n, 8, 128), f32),
            pltpu.VMEM((tokens, 128), f32),
            pltpu.VMEM((tokens, 128), f32),
            pltpu.VMEM((SLOTS, 2, 2 * half, wide), bf16),
            pltpu.VMEM((2, tokens, wide), f32),
            pltpu.VMEM((tokens, wide), bf16),
            pltpu.VMEM((SLOTS, wide, 2 * half), bf16),
            pltpu.VMEM((STEPS, tokens, half), bf16),
            pltpu.VMEM((STEPS, tokens, half), bf16),
            pltpu.VMEM((Z * H, tokens, half), bf16),
            pltpu.VMEM((Z * H, tokens, half), bf16),
            pltpu.VMEM((Z * H, tokens, half), bf16),
            pltpu.VMEM((2, Z * H, tokens, half), bf16),
            pltpu.VMEM((2, tokens, half), bf16),
            pltpu.VMEM((2, tokens, half), bf16),
            pltpu.VMEM((2, tokens, half), f32),
            pltpu.VMEM((H, tokens, half), bf16),
            dma,
            dma((H,)),
            dma((SLOTS, 2, 2)),
            dma((SLOTS, 2)),
            dma((n,)),
            dma((Z * X,)),
            dma((Z,)),
            dma((Z,)),
            dma((Z,)),
            dma((STEPS, 2)),
            dma((Z * H,)),
            dma((Z * H,)),
            dma((Z * H,)),
            dma((STEPS,)),
            dma((2,)),
            dma((STEPS,)),
            dma((STEPS,)),
            dma((Z * H,)),
            dma((Z * H,)),
            dma((Z * H,)),
            dma((2, Z * H)),
            dma((2,)),
            dma((2,)),
        ],
        compiler_params=pltpu.CompilerParams(
            collective_id=0, has_side_effects=True, vmem_limit_bytes=62 * 2**20
        ),
    )(activations, norm_gain.reshape(feat // 128, 128), gate_weight, up_weight, down_weight)


def solution(mesh):
    in_specs = (P("groups", "row"), P("row"), P(None, "row"), P(None, "row"), P("row", None))
    out_specs = P("groups", "row")
    n = mesh.shape["row"]

    def per_device(activations, norm_gain, gate_weight, up_weight, down_weight):
        tokens, feat = activations.shape
        fits = (
            n == 2 * Z * X
            and tokens % 128 == 0
            and tokens // 128 <= 8
            and feat % (128 * H) == 0
            and gate_weight.shape[1] % 128 == 0
        )
        body = fused if fits else plain
        return body(activations, norm_gain, gate_weight, up_weight, down_weight)

    return jax.shard_map(
        per_device, mesh=mesh, in_specs=in_specs, out_specs=out_specs, check_vma=False
    )
```

```python
import jax
import jax.numpy as jnp
from jax import lax
from jax.experimental import pallas as pl
from jax.experimental.pallas import tpu as pltpu
from jax.sharding import PartitionSpec as P

D = 8192
Z, X, H = 4, 2, 2
STEPS = Z * X * H
SLOTS = 4
MESH = pl.DeviceIdType.MESH


GATHER_END = (0, 1, 4, 2, 5, 3, 8, 6, 9, 7, 12, 10, 13, 11, 14, 15)
GATHER_MID = (4, 5, 8, 0, 6, 9, 1, 12, 7, 13, 2, 3, 15, 10, 11, 14)
LATE, LATE_AT = 12, 10
INNER_END, INNER_MID, OUTER_MID = 5, 8, 12
REDUCE_END = (14, 15, 10, 13, 11, 6, 12, 7, 2, 8, 3, 9, 4, 5, 0, 1)
REDUCE_MID = (14, 3, 11, 2, 15, 10, 6, 7, 13, 12, 1, 8, 0, 9, 4, 5)


def plain(activations, norm_gain, gate_weight, up_weight, down_weight):
    float_rows = activations.astype(jnp.float32)
    square_sums = lax.psum(jnp.sum(float_rows * float_rows, axis=1), "row")
    inv_scale = lax.rsqrt(square_sums / D + 1e-05)
    normed = (float_rows * inv_scale[:, None] * norm_gain.astype(jnp.float32)[None, :]).astype(
        jnp.bfloat16
    )
    shard_rows = lax.all_gather(normed, "row", axis=1, tiled=True)
    gate_proj = jnp.dot(shard_rows, gate_weight, preferred_element_type=jnp.float32)
    up_proj = jnp.dot(shard_rows, up_weight, preferred_element_type=jnp.float32)
    hidden = (jax.nn.silu(gate_proj) * up_proj).astype(jnp.bfloat16)
    reduced = lax.psum_scatter(
        lax.dot_general(
            down_weight, hidden, (((0,), (1,)), ((), ())), preferred_element_type=jnp.float32
        ),
        "row",
        scatter_dimension=0,
        tiled=True,
    )
    return reduced.T.astype(jnp.bfloat16)


def kernel(
    act, gain, gate_w, up_w, down_w, out,
    act_buf, gathered, stats, squares, inv, w_buf, acc, hidden, dw_buf,
    core_out, core_in, x_out, x_in, z_out, z_in, e_out, e_in, total, result,
    act_sem, out_sem, w_sem, dw_sem, s_recv, s_partner, s_core, s_x, s_z,
    g_recv, g_z, g_x, g_core,
    core_send, core_recv, x_send, x_recv, z_send, z_recv, e_send, e_recv,
):
    n = 2 * Z * X
    bf16, f32 = jnp.bfloat16, jnp.float32
    me = lax.axis_index("row")
    c = lax.rem(me, 2)
    x = lax.rem(me // 2, X)
    z = me // (2 * X)
    tokens, wide = hidden.shape
    feat = act_buf.shape[1]
    half = feat // H
    end = (z == 0) | (z == Z - 1)
    mid = jnp.logical_not(end)
    low = z < Z // 2
    partner = me + 1 - 2 * c
    across = me + 2 - 4 * x
    above = jnp.minimum(me + 2 * X, n - 1)
    below = jnp.maximum(me - 2 * X, 0)
    inner = jnp.where(low, above, below)
    outer = jnp.where(low, below, above)
    my_cols = pl.ds(pl.multiple_of(c * half, half), half)

    def remote(src, dst, send, recv, target):
        return pltpu.make_async_remote_copy(
            src_ref=src, dst_ref=dst, send_sem=send, recv_sem=recv,
            device_id={"row": target}, device_id_type=MESH,
        )

    def pick(table, index):
        value = jnp.int32(table[0])
        for at in range(1, len(table)):
            value = jnp.where(index == at, jnp.int32(table[at]), value)
        return value

    def gather_code(s):
        return jnp.where(end, pick(GATHER_END, s), pick(GATHER_MID, s))

    def reduce_code(i):
        return jnp.where(end, pick(REDUCE_END, i), pick(REDUCE_MID, i))

    def by_z(plane, h):
        return (h == 1) & jnp.where(end, plane == Z - 1, (plane == 0) | (plane == 2))

    def decode(code):
        plane = code // 4
        p = jnp.where(low, plane, Z - 1 - plane)
        other = lax.rem(code // 2, 2)
        h = lax.rem(code, 2)
        chip = p * X + jnp.where(other == 1, 1 - x, x)
        return other == 0, h, plane, p, chip

    def weights(s):
        _, h, _, _, chip = decode(gather_code(s))
        slot = lax.rem(s, SLOTS)
        copies = []
        for i, w in enumerate((gate_w, up_w)):
            for core in range(2):
                start = (chip * 2 + core) * feat + h * half
                rows = pl.ds(pl.multiple_of(start, half), half)
                copies.append(
                    pltpu.make_async_copy(
                        w.at[rows],
                        w_buf.at[slot, i, pl.ds(core * half, half)],
                        w_sem.at[slot],
                    )
                )
        return copies

    def down(i):
        _, h, _, _, chip = decode(reduce_code(i))
        slot = lax.rem(i, SLOTS)
        copies = []
        for mine in range(2):
            core = c if mine else 1 - c
            start = (chip * 2 + core) * feat + h * half
            cols = pl.ds(pl.multiple_of(start, half), half)
            copies.append(
                pltpu.make_async_copy(
                    down_w.at[:, cols],
                    dw_buf.at[slot, :, pl.ds(mine * half, half)],
                    dw_sem.at[slot],
                )
            )
        return copies

    own = pltpu.make_async_copy(act, act_buf, act_sem)
    own.start()
    for copy in weights(jnp.int32(0)):
        copy.start()

    barrier = pltpu.get_barrier_semaphore()

    def greet(target):
        pl.semaphore_signal(barrier, inc=1, device_id={"row": target}, device_id_type=MESH)

    greet(partner)
    greet(across)

    @pl.when(z < Z - 1)
    def _():
        greet(above)

    @pl.when(z > 0)
    def _():
        greet(below)

    blocks = tokens // 128
    mine_at = (z * X + x) * H
    gains = gain[...].astype(f32)
    with jax.named_scope("own_wait"):
        own.wait()
    for s in range(1, SLOTS):
        for copy in weights(jnp.int32(s)):
            copy.start()
    for h in range(H):
        for j in range(half // 128):
            at = h * (half // 128) + j
            part = act_buf[:, at * 128 : (at + 1) * 128].astype(f32) * gains[at : at + 1, :]
            cols = pl.ds(pl.multiple_of(c * half + j * 128, 128), 128)
            gathered[mine_at + h, :, cols] = part.astype(bf16)
    with jax.named_scope("barrier_wait"):
        pl.semaphore_wait(barrier, jnp.where(end, 3, 4))

    def pass_core(at):
        ref = gathered.at[at, :, my_cols]
        return remote(ref, ref, g_core, g_recv.at[at, c], partner)

    def passed(chip, h, send, target):
        ref, recv = gathered.at[chip * H + h, :, my_cols], g_recv.at[chip * H + h, c]
        return remote(ref, ref, send, recv, target)

    def pass_x(chip, h):
        return passed(chip, h, g_x, across)

    def pass_up(chip, h):
        return passed(chip, h, g_z, above)

    def pass_down(chip, h):
        return passed(chip, h, g_z, below)

    def tell(chip, send, recv, target):
        ref = stats.at[chip, c]
        return remote(ref, ref, send, recv, target)

    def tell_on(in_line, p, chip):
        tell(chip, s_core, s_partner, partner).start()

        @pl.when(in_line)
        def _():
            tell(chip, s_x, s_recv.at[chip], across).start()

        @pl.when(in_line & (p <= z) & (z < Z - 1))
        def _():
            tell(chip, s_z, s_recv.at[chip], above).start()

        @pl.when(in_line & (p >= z) & (z > 0))
        def _():
            tell(chip, s_z, s_recv.at[chip], below).start()

    def extra(to_inner):
        plane = jnp.where(end, 0, 1) if to_inner else jnp.int32(Z - 1)
        p = jnp.where(low, plane, Z - 1 - plane)
        at = (p * X + 1 - x) * H + 1
        ref, recv = gathered.at[at, :, my_cols], g_recv.at[at, c]
        return remote(ref, ref, g_z, recv, inner if to_inner else outer)

    def arrived(s, core):
        _, h, _, _, chip = decode(gather_code(s))
        at = chip * H + h
        cols = pl.ds(pl.multiple_of(core * half, half), half)
        ref = gathered.at[at, :, cols]
        pltpu.make_async_copy(ref, ref, g_recv.at[at, core]).wait()

    def forward(s):
        in_line, h, plane, p, chip = decode(gather_code(s))
        pass_core(chip * H + h).start()
        late = mid & (gather_code(s) == LATE)

        @pl.when(in_line & jnp.logical_not(by_z(plane, h) | late))
        def _():
            pass_x(chip, h).start()

        @pl.when(in_line & (p <= z) & (z < Z - 1))
        def _():
            pass_up(chip, h).start()

        @pl.when(in_line & (p >= z) & (z > 0))
        def _():
            pass_down(chip, h).start()

        @pl.when(mid & (s == LATE_AT))
        def _():
            _, late_h, _, _, late_chip = decode(jnp.int32(LATE))
            pass_x(late_chip, late_h).start()

        @pl.when((h == 1) & (s >= H))
        def _():
            ref = stats.at[chip, c]
            pltpu.make_async_copy(ref, ref, s_recv.at[chip]).wait()
            tell_on(in_line, p, chip)

        @pl.when(s == jnp.where(end, INNER_END, INNER_MID))
        def _():
            extra(1).start()

        @pl.when(mid & (s == OUTER_MID))
        def _():
            extra(0).start()

    for h in range(H):
        forward(jnp.int32(h))

    rows = act_buf[...].astype(f32)
    sums = jnp.sum(rows * rows, axis=1, keepdims=True)
    squares[...] = jnp.broadcast_to(sums, (tokens, 128))
    for b in range(blocks):
        stats[me // 2, c, b : b + 1, :] = squares[b * 128 : (b + 1) * 128, :].T[0:1, :]

    tell_on(True, z, z * X + x)
    acc[...] = jnp.zeros_like(acc)

    def gather_step(s, carry):
        _, h, _, _, chip = decode(gather_code(s))
        slot = lax.rem(s, SLOTS)
        at = chip * H + h
        even = lax.rem(s, 2) == 0

        @pl.when((s >= H - 1) & (s < STEPS - 1) & (mid | jnp.logical_not(even)))
        def _():
            with jax.named_scope("link_wait0"):
                arrived(s + 1, c)
            forward(s + 1)

        @pl.when(end & (s >= H - 1) & (s < STEPS - 1) & jnp.logical_not(even))
        def _():
            with jax.named_scope("link_wait1"):
                arrived(s + 2, c)
            forward(s + 2)

        with jax.named_scope("weight_wait"):
            pltpu.make_async_copy(w_buf.at[slot], w_buf.at[slot], w_sem.at[slot]).wait()
        with jax.named_scope("partner_wait"):
            arrived(s, 1 - c)
        for i in range(2):
            acc[i] += jnp.dot(gathered[at], w_buf[slot, i], preferred_element_type=f32)

        @pl.when(s < STEPS - SLOTS)
        def _():
            for copy in weights(s + SLOTS):
                copy.start()

        @pl.when((s >= STEPS // 2) & (s < STEPS // 2 + SLOTS))
        def _():
            for copy in down(s - STEPS // 2):
                copy.start()

        return carry

    with jax.named_scope("gather"):
        lax.fori_loop(0, STEPS, gather_step, 0)

    theirs = stats.at[:, 1 - c]
    pltpu.make_async_copy(theirs, theirs, s_partner).wait()
    sums = stats[0, 0]
    for origin in range(1, n):
        sums = sums + stats[origin // 2, origin % 2]
    scale = lax.rsqrt(sums / (n * feat) + 1e-05)
    for b in range(blocks):
        inv[b * 128 : (b + 1) * 128, :] = jnp.broadcast_to(scale[b : b + 1, :], (128, 128)).T

    def activate(t, carry):
        cols = pl.ds(pl.multiple_of(t * 128, 128), 128)
        by_two = 0.5 * (acc[0, :, cols] * inv[...])
        up = acc[1, :, cols] * inv[...]
        hidden[:, cols] = (by_two * (1.0 + jnp.tanh(by_two)) * up).astype(bf16)
        return carry

    with jax.named_scope("activation"):
        lax.fori_loop(0, wide // 128, activate, 0)

    def core_copy(i):
        return remote(core_out.at[i], core_in.at[i], core_send, core_recv.at[i], partner)

    def x_copy(at):
        return remote(x_out.at[at], x_in.at[at], x_send, x_recv.at[at], across)

    def z_copy(at, side, target):
        return remote(z_out.at[at], z_in.at[side, at], z_send, z_recv.at[side, at], target)

    def e_copy(side, target):
        return remote(e_out.at[side], e_in.at[side], e_send, e_recv.at[side], target)

    def out_copy(h):
        cols = pl.ds(pl.multiple_of(h * half, half), half)
        return pltpu.make_async_copy(result.at[h], out.at[:, cols], out_sem.at[h])

    def finish(j):
        in_line, h, plane, p, chip = decode(reduce_code(j))
        cross = jnp.logical_not(in_line)
        special = by_z(plane, h)
        at = p * H + h
        slot = lax.rem(j, 2)
        from_inner = cross & (h == 1) & (p == z)
        from_outer = cross & (h == 1) & mid & (plane == Z - 1)
        with jax.named_scope("core_wait"):
            core_copy(j).wait_recv()
        total[slot] += core_in[j].astype(f32)

        @pl.when(in_line & jnp.logical_not(special))
        def _():
            with jax.named_scope("x_wait"):
                x_copy(at).wait_recv()
            total[slot] += x_in[at].astype(f32)

        @pl.when(in_line & (z > 0) & (p >= z))
        def _():
            with jax.named_scope("zb_wait"):
                z_copy(at, 0, above).wait_recv()
            total[slot] += z_in[0, at].astype(f32)

        @pl.when(in_line & (z < Z - 1) & (p <= z))
        def _():
            with jax.named_scope("za_wait"):
                z_copy(at, 1, below).wait_recv()
            total[slot] += z_in[1, at].astype(f32)

        @pl.when(jnp.where(low, from_outer, from_inner))
        def _():
            with jax.named_scope("e_wait"):
                e_copy(0, above).wait_recv()
            total[slot] += e_in[0].astype(f32)

        @pl.when(jnp.where(low, from_inner, from_outer))
        def _():
            with jax.named_scope("e_wait"):
                e_copy(1, below).wait_recv()
            total[slot] += e_in[1].astype(f32)

        @pl.when(in_line & (p == z))
        def _():
            result[h] = total[slot].astype(bf16)
            out_copy(h).start()

        @pl.when(in_line & (p != z))
        def _():
            z_out[at] = total[slot].astype(bf16)

        @pl.when(in_line & (p > z))
        def _():
            z_copy(at, 0, above).start()

        @pl.when(in_line & (p < z))
        def _():
            z_copy(at, 1, below).start()

        @pl.when(cross & jnp.logical_not(special))
        def _():
            x_out[at] = total[slot].astype(bf16)
            x_copy(at).start()

        @pl.when(cross & special & (p > z))
        def _():
            e_out[0] = total[slot].astype(bf16)
            e_copy(0, above).start()

        @pl.when(cross & special & (p < z))
        def _():
            e_out[1] = total[slot].astype(bf16)
            e_copy(1, below).start()

    def sent(ref, count, sem):
        ref = ref.at[pl.ds(0, count)]
        pltpu.make_async_copy(ref, ref, sem).wait()

    def drain_gather():
        pieces, rows = gathered.at[:, :, my_cols], stats.at[:, c]
        sent(pieces, STEPS, g_core)
        sent(rows, Z * X, s_core)
        sent(rows, Z, s_x)

        @pl.when(end)
        def _():
            sent(pieces, 7, g_x)
            sent(pieces, 3, g_z)
            sent(rows, 1, s_z)

        @pl.when(mid)
        def _():
            sent(pieces, 6, g_x)
            sent(pieces, 12, g_z)
            sent(rows, 5, s_z)

    def reduce_step(i, carry):
        @pl.when(i < STEPS)
        def _():
            slot = lax.rem(i, SLOTS)
            pltpu.make_async_copy(dw_buf.at[slot], dw_buf.at[slot], dw_sem.at[slot]).wait()
            part = jnp.dot(hidden[...], dw_buf[slot], preferred_element_type=f32)
            core_out[i] = part[:, :half].astype(bf16)
            core_copy(i).start()
            total[lax.rem(i, 2)] = part[:, half:]

        @pl.when(i < STEPS - SLOTS)
        def _():
            for copy in down(i + SLOTS):
                copy.start()

        @pl.when(i > 0)
        def _():
            with jax.named_scope("finish"):
                finish(i - 1)

        @pl.when(i == STEPS - 2)
        def _():
            drain_gather()

        return carry

    with jax.named_scope("reduce"):
        lax.fori_loop(0, STEPS + 1, reduce_step, 0)

    sent(core_out, STEPS, core_send)
    sent(z_out, (Z - 1) * H, z_send)

    @pl.when(end)
    def _():
        sent(x_out, 7, x_send)
        sent(e_out, 1, e_send)

    @pl.when(mid)
    def _():
        sent(x_out, 6, x_send)
        sent(e_out, 2, e_send)

    for h in range(H):
        out_copy(h).wait()


def fused(activations, norm_gain, gate_weight, up_weight, down_weight):
    tokens, feat = activations.shape
    wide = gate_weight.shape[1]
    n, half = 2 * Z * X, feat // H
    bf16, f32 = jnp.bfloat16, jnp.float32
    anywhere = pl.BlockSpec(memory_space=pl.ANY)
    vmem = pl.BlockSpec(memory_space=pltpu.VMEM)
    dma = pltpu.SemaphoreType.DMA
    return pl.pallas_call(
        kernel,
        out_shape=jax.ShapeDtypeStruct((tokens, feat), bf16),
        in_specs=[anywhere, vmem, anywhere, anywhere, anywhere],
        out_specs=anywhere,
        scratch_shapes=[
            pltpu.VMEM((tokens, feat), bf16),
            pltpu.VMEM((STEPS, tokens, 2 * half), bf16),
            pltpu.VMEM((Z * X, 2, 8, 128), f32),
            pltpu.VMEM((tokens, 128), f32),
            pltpu.VMEM((tokens, 128), f32),
            pltpu.VMEM((SLOTS, 2, 2 * half, wide), bf16),
            pltpu.VMEM((2, tokens, wide), f32),
            pltpu.VMEM((tokens, wide), bf16),
            pltpu.VMEM((SLOTS, wide, 2 * half), bf16),
            pltpu.VMEM((STEPS, tokens, half), bf16),
            pltpu.VMEM((STEPS, tokens, half), bf16),
            pltpu.VMEM((Z * H, tokens, half), bf16),
            pltpu.VMEM((Z * H, tokens, half), bf16),
            pltpu.VMEM((Z * H, tokens, half), bf16),
            pltpu.VMEM((2, Z * H, tokens, half), bf16),
            pltpu.VMEM((2, tokens, half), bf16),
            pltpu.VMEM((2, tokens, half), bf16),
            pltpu.VMEM((2, tokens, half), f32),
            pltpu.VMEM((H, tokens, half), bf16),
            dma,
            dma((H,)),
            dma((SLOTS,)),
            dma((SLOTS,)),
            dma((Z * X,)),
            dma,
            dma,
            dma,
            dma,
            dma((STEPS, 2)),
            dma,
            dma,
            dma,
            dma,
            dma((STEPS,)),
            dma,
            dma((Z * H,)),
            dma,
            dma((2, Z * H)),
            dma,
            dma((2,)),
        ],
        compiler_params=pltpu.CompilerParams(
            collective_id=0, has_side_effects=True, vmem_limit_bytes=62 * 2**20
        ),
    )(activations, norm_gain.reshape(feat // 128, 128), gate_weight, up_weight, down_weight)


def solution(mesh):
    in_specs = (P("groups", "row"), P("row"), P(None, "row"), P(None, "row"), P("row", None))
    out_specs = P("groups", "row")
    n = mesh.shape["row"]

    def per_device(activations, norm_gain, gate_weight, up_weight, down_weight):
        tokens, feat = activations.shape
        fits = (
            n == 2 * Z * X
            and tokens % 128 == 0
            and tokens // 128 <= 8
            and feat % (128 * H) == 0
            and gate_weight.shape[1] % 128 == 0
        )
        body = fused if fits else plain
        return body(activations, norm_gain, gate_weight, up_weight, down_weight)

    return jax.shard_map(
        per_device, mesh=mesh, in_specs=in_specs, out_specs=out_specs, check_vma=False
    )
```

```python
import jax
import jax.numpy as jnp
from jax import lax
from jax.experimental import pallas as pl
from jax.experimental.pallas import tpu as pltpu
from jax.sharding import PartitionSpec as P

D = 8192
Z, X, H = 4, 2, 2
STEPS = Z * X * H
SLOTS = 4
COLS = 256
MESH = pl.DeviceIdType.MESH


GATHER_END = (0, 1, 4, 2, 5, 3, 8, 6, 9, 7, 12, 10, 13, 11, 14, 15)
GATHER_MID = (4, 5, 8, 0, 6, 9, 1, 12, 7, 13, 2, 3, 15, 10, 11, 14)
LATE, LATE_AT = 12, 10
INNER_END, INNER_MID, OUTER_MID = 5, 8, 12
REDUCE_END = (14, 15, 10, 13, 11, 6, 12, 7, 2, 8, 3, 9, 4, 5, 0, 1)
REDUCE_MID = (14, 3, 11, 2, 15, 10, 6, 7, 13, 12, 1, 8, 0, 9, 4, 5)


def plain(activations, norm_gain, gate_weight, up_weight, down_weight):
    float_rows = activations.astype(jnp.float32)
    square_sums = lax.psum(jnp.sum(float_rows * float_rows, axis=1), "row")
    inv_scale = lax.rsqrt(square_sums / D + 1e-05)
    normed = (float_rows * inv_scale[:, None] * norm_gain.astype(jnp.float32)[None, :]).astype(
        jnp.bfloat16
    )
    shard_rows = lax.all_gather(normed, "row", axis=1, tiled=True)
    gate_proj = jnp.dot(shard_rows, gate_weight, preferred_element_type=jnp.float32)
    up_proj = jnp.dot(shard_rows, up_weight, preferred_element_type=jnp.float32)
    hidden = (jax.nn.silu(gate_proj) * up_proj).astype(jnp.bfloat16)
    reduced = lax.psum_scatter(
        lax.dot_general(
            down_weight, hidden, (((0,), (1,)), ((), ())), preferred_element_type=jnp.float32
        ),
        "row",
        scatter_dimension=0,
        tiled=True,
    )
    return reduced.T.astype(jnp.bfloat16)


def kernel(
    act, gain, gate_w, up_w, down_w, out,
    act_buf, gathered, stats, squares, inv, w_buf, acc, hidden, dw_buf,
    core_out, core_in, x_out, x_in, z_out, z_in, e_out, e_in, total,
    act_sem, w_sem, dw_sem, s_recv, s_partner, s_core, s_x, s_z,
    g_recv, g_z, g_x, g_core,
    core_send, core_recv, x_send, x_recv, z_send, z_recv, e_send, e_recv,
):
    n = 2 * Z * X
    bf16, f32 = jnp.bfloat16, jnp.float32
    me = lax.axis_index("row")
    c = lax.rem(me, 2)
    x = lax.rem(me // 2, X)
    z = me // (2 * X)
    tokens, wide = hidden.shape
    feat = act_buf.shape[1]
    half = feat // H
    end = (z == 0) | (z == Z - 1)
    mid = jnp.logical_not(end)
    low = z < Z // 2
    partner = me + 1 - 2 * c
    across = me + 2 - 4 * x
    above = jnp.minimum(me + 2 * X, n - 1)
    below = jnp.maximum(me - 2 * X, 0)
    inner = jnp.where(low, above, below)
    outer = jnp.where(low, below, above)
    my_cols = pl.ds(pl.multiple_of(c * half, half), half)

    def remote(src, dst, send, recv, target):
        return pltpu.make_async_remote_copy(
            src_ref=src, dst_ref=dst, send_sem=send, recv_sem=recv,
            device_id={"row": target}, device_id_type=MESH,
        )

    def pick(table, index):
        value = jnp.int32(table[0])
        for at in range(1, len(table)):
            value = jnp.where(index == at, jnp.int32(table[at]), value)
        return value

    def gather_code(s):
        return jnp.where(end, pick(GATHER_END, s), pick(GATHER_MID, s))

    def reduce_code(i):
        return jnp.where(end, pick(REDUCE_END, i), pick(REDUCE_MID, i))

    def by_z(plane, h):
        return (h == 1) & jnp.where(end, plane == Z - 1, (plane == 0) | (plane == 2))

    def decode(code):
        plane = code // 4
        p = jnp.where(low, plane, Z - 1 - plane)
        other = lax.rem(code // 2, 2)
        h = lax.rem(code, 2)
        chip = p * X + jnp.where(other == 1, 1 - x, x)
        return other == 0, h, plane, p, chip

    def weights(s):
        _, h, _, _, chip = decode(gather_code(s))
        slot = lax.rem(s, SLOTS)
        copies = []
        for i, w in enumerate((gate_w, up_w)):
            for core in range(2):
                start = (chip * 2 + core) * feat + h * half
                rows = pl.ds(pl.multiple_of(start, half), half)
                copies.append(
                    pltpu.make_async_copy(
                        w.at[rows],
                        w_buf.at[slot, i, pl.ds(core * half, half)],
                        w_sem.at[slot],
                    )
                )
        return copies

    def down(i):
        _, h, _, _, chip = decode(reduce_code(i))
        slot = lax.rem(i, SLOTS)
        copies = []
        for mine in range(2):
            core = c if mine else 1 - c
            start = (chip * 2 + core) * feat + h * half
            cols = pl.ds(pl.multiple_of(start, half), half)
            copies.append(
                pltpu.make_async_copy(
                    down_w.at[:, cols],
                    dw_buf.at[slot, :, pl.ds(mine * half, half)],
                    dw_sem.at[slot],
                )
            )
        return copies

    own = pltpu.make_async_copy(act, act_buf, act_sem)
    own.start()
    for copy in weights(jnp.int32(0)):
        copy.start()

    barrier = pltpu.get_barrier_semaphore()

    def greet(target):
        pl.semaphore_signal(barrier, inc=1, device_id={"row": target}, device_id_type=MESH)

    greet(partner)
    greet(across)

    @pl.when(z < Z - 1)
    def _():
        greet(above)

    @pl.when(z > 0)
    def _():
        greet(below)

    blocks = tokens // 128
    mine_at = (z * X + x) * H
    gains = gain[...].astype(f32)
    with jax.named_scope("own_wait"):
        own.wait()
    for s in range(1, SLOTS):
        for copy in weights(jnp.int32(s)):
            copy.start()
    for h in range(H):
        for j in range(half // 128):
            at = h * (half // 128) + j
            part = act_buf[:, at * 128 : (at + 1) * 128].astype(f32) * gains[at : at + 1, :]
            cols = pl.ds(pl.multiple_of(c * half + j * 128, 128), 128)
            gathered[mine_at + h, :, cols] = part.astype(bf16)
    with jax.named_scope("barrier_wait"):
        pl.semaphore_wait(barrier, jnp.where(end, 3, 4))

    def pass_core(at):
        ref = gathered.at[at, :, my_cols]
        return remote(ref, ref, g_core, g_recv.at[at, c], partner)

    def passed(chip, h, send, target):
        ref, recv = gathered.at[chip * H + h, :, my_cols], g_recv.at[chip * H + h, c]
        return remote(ref, ref, send, recv, target)

    def pass_x(chip, h):
        return passed(chip, h, g_x, across)

    def pass_up(chip, h):
        return passed(chip, h, g_z, above)

    def pass_down(chip, h):
        return passed(chip, h, g_z, below)

    def tell(chip, send, recv, target):
        ref = stats.at[chip, c]
        return remote(ref, ref, send, recv, target)

    def tell_on(in_line, p, chip):
        tell(chip, s_core, s_partner, partner).start()

        @pl.when(in_line)
        def _():
            tell(chip, s_x, s_recv.at[chip], across).start()

        @pl.when(in_line & (p <= z) & (z < Z - 1))
        def _():
            tell(chip, s_z, s_recv.at[chip], above).start()

        @pl.when(in_line & (p >= z) & (z > 0))
        def _():
            tell(chip, s_z, s_recv.at[chip], below).start()

    def extra(to_inner):
        plane = jnp.where(end, 0, 1) if to_inner else jnp.int32(Z - 1)
        p = jnp.where(low, plane, Z - 1 - plane)
        at = (p * X + 1 - x) * H + 1
        ref, recv = gathered.at[at, :, my_cols], g_recv.at[at, c]
        return remote(ref, ref, g_z, recv, inner if to_inner else outer)

    def arrived(s, core):
        _, h, _, _, chip = decode(gather_code(s))
        at = chip * H + h
        cols = pl.ds(pl.multiple_of(core * half, half), half)
        ref = gathered.at[at, :, cols]
        pltpu.make_async_copy(ref, ref, g_recv.at[at, core]).wait()

    def forward(s):
        in_line, h, plane, p, chip = decode(gather_code(s))
        pass_core(chip * H + h).start()
        late = mid & (gather_code(s) == LATE)

        @pl.when(in_line & jnp.logical_not(by_z(plane, h) | late))
        def _():
            pass_x(chip, h).start()

        @pl.when(in_line & (p <= z) & (z < Z - 1))
        def _():
            pass_up(chip, h).start()

        @pl.when(in_line & (p >= z) & (z > 0))
        def _():
            pass_down(chip, h).start()

        @pl.when(mid & (s == LATE_AT))
        def _():
            _, late_h, _, _, late_chip = decode(jnp.int32(LATE))
            pass_x(late_chip, late_h).start()

        @pl.when((h == 1) & (s >= H))
        def _():
            ref = stats.at[chip, c]
            pltpu.make_async_copy(ref, ref, s_recv.at[chip]).wait()
            tell_on(in_line, p, chip)

        @pl.when(s == jnp.where(end, INNER_END, INNER_MID))
        def _():
            extra(1).start()

        @pl.when(mid & (s == OUTER_MID))
        def _():
            extra(0).start()

    for h in range(H):
        forward(jnp.int32(h))

    rows = act_buf[...].astype(f32)
    sums = jnp.sum(rows * rows, axis=1, keepdims=True)
    squares[...] = jnp.broadcast_to(sums, (tokens, 128))
    for b in range(blocks):
        stats[me // 2, c, b : b + 1, :] = squares[b * 128 : (b + 1) * 128, :].T[0:1, :]

    tell_on(True, z, z * X + x)
    acc[...] = jnp.zeros_like(acc)

    def gather_step(s, carry):
        _, h, _, _, chip = decode(gather_code(s))
        slot = lax.rem(s, SLOTS)
        at = chip * H + h
        fresh = (s == H) | (end & (s > H) & (lax.rem(s, 2) == 0))

        @pl.when(fresh)
        def _():
            with jax.named_scope("link_wait0"):
                arrived(s, c)
            forward(s)

        @pl.when(fresh | (mid & (s > H)))
        def _():
            with jax.named_scope("link_wait1"):
                arrived(s + 1, c)
            forward(s + 1)

        with jax.named_scope("weight_wait"):
            pltpu.make_async_copy(w_buf.at[slot], w_buf.at[slot], w_sem.at[slot]).wait()

        def lane(core):
            cols = pl.ds(pl.multiple_of(core * half, half), half)
            for i in range(2):
                acc[i] += jnp.dot(
                    gathered[at, :, cols], w_buf[slot, i, cols, :], preferred_element_type=f32
                )

        @pl.when(fresh)
        def _():
            lane(c)
            with jax.named_scope("partner_wait0"):
                arrived(s, 1 - c)
            lane(1 - c)

        @pl.when(jnp.logical_not(fresh))
        def _():
            with jax.named_scope("partner_wait"):
                arrived(s, 1 - c)
            for i in range(2):
                acc[i] += jnp.dot(gathered[at], w_buf[slot, i], preferred_element_type=f32)

        @pl.when(s < STEPS - SLOTS)
        def _():
            for copy in weights(s + SLOTS):
                copy.start()

        @pl.when((s >= STEPS // 2) & (s < STEPS // 2 + SLOTS))
        def _():
            for copy in down(s - STEPS // 2):
                copy.start()

        return carry

    with jax.named_scope("gather"):
        lax.fori_loop(0, STEPS - 1, gather_step, 0)

    theirs = stats.at[:, 1 - c]
    pltpu.make_async_copy(theirs, theirs, s_partner).wait()
    sums = stats[0, 0]
    for origin in range(1, n):
        sums = sums + stats[origin // 2, origin % 2]
    scale = lax.rsqrt(sums / (n * feat) + 1e-05)
    for b in range(blocks):
        inv[b * 128 : (b + 1) * 128, :] = jnp.broadcast_to(scale[b : b + 1, :], (128, 128)).T

    with jax.named_scope("activation"):
        last = STEPS - 1
        _, h, _, _, chip = decode(gather_code(last))
        slot, at = last % SLOTS, chip * H + h
        pltpu.make_async_copy(w_buf.at[slot], w_buf.at[slot], w_sem.at[slot]).wait()
        arrived(last, 1 - c)
        for t in range(wide // COLS):
            cols = slice(t * COLS, (t + 1) * COLS)
            gate, up = (
                acc[i, :, cols]
                + jnp.dot(gathered[at], w_buf[slot, i, :, cols], preferred_element_type=f32)
                for i in range(2)
            )
            for q in range(0, COLS, 128):
                by_two = 0.5 * (gate[:, q : q + 128] * inv[...])
                value = by_two * (1.0 + jnp.tanh(by_two)) * (up[:, q : q + 128] * inv[...])
                hidden[:, t * COLS + q : t * COLS + q + 128] = value.astype(bf16)

    def core_copy(i):
        return remote(core_out.at[i], core_in.at[i], core_send, core_recv.at[i], partner)

    def x_copy(at):
        return remote(x_out.at[at], x_in.at[at], x_send, x_recv.at[at], across)

    def z_copy(at, side, target):
        return remote(z_out.at[at], z_in.at[side, at], z_send, z_recv.at[side, at], target)

    def e_copy(side, target):
        return remote(e_out.at[side], e_in.at[side], e_send, e_recv.at[side], target)

    def finish(j):
        in_line, h, plane, p, chip = decode(reduce_code(j))
        cross = jnp.logical_not(in_line)
        special = by_z(plane, h)
        at = p * H + h
        slot = lax.rem(j, 2)
        from_inner = cross & (h == 1) & (p == z)
        from_outer = cross & (h == 1) & mid & (plane == Z - 1)
        with jax.named_scope("core_wait"):
            core_copy(j).wait_recv()
        total[slot] += core_in[j].astype(f32)

        @pl.when(in_line & jnp.logical_not(special))
        def _():
            with jax.named_scope("x_wait"):
                x_copy(at).wait_recv()
            total[slot] += x_in[at].astype(f32)

        @pl.when(in_line & (z > 0) & (p >= z))
        def _():
            with jax.named_scope("zb_wait"):
                z_copy(at, 0, above).wait_recv()
            total[slot] += z_in[0, at].astype(f32)

        @pl.when(in_line & (z < Z - 1) & (p <= z))
        def _():
            with jax.named_scope("za_wait"):
                z_copy(at, 1, below).wait_recv()
            total[slot] += z_in[1, at].astype(f32)

        @pl.when(jnp.where(low, from_outer, from_inner))
        def _():
            with jax.named_scope("e_wait"):
                e_copy(0, above).wait_recv()
            total[slot] += e_in[0].astype(f32)

        @pl.when(jnp.where(low, from_inner, from_outer))
        def _():
            with jax.named_scope("e_wait"):
                e_copy(1, below).wait_recv()
            total[slot] += e_in[1].astype(f32)

        @pl.when(in_line & (p == z))
        def _():
            cols = pl.ds(pl.multiple_of(h * half, half), half)
            out[:, cols] = total[slot].astype(bf16)

        @pl.when(in_line & (p != z))
        def _():
            z_out[at] = total[slot].astype(bf16)

        @pl.when(in_line & (p > z))
        def _():
            z_copy(at, 0, above).start()

        @pl.when(in_line & (p < z))
        def _():
            z_copy(at, 1, below).start()

        @pl.when(cross & jnp.logical_not(special))
        def _():
            x_out[at] = total[slot].astype(bf16)
            x_copy(at).start()

        @pl.when(cross & special & (p > z))
        def _():
            e_out[0] = total[slot].astype(bf16)
            e_copy(0, above).start()

        @pl.when(cross & special & (p < z))
        def _():
            e_out[1] = total[slot].astype(bf16)
            e_copy(1, below).start()

    def sent(ref, count, sem):
        ref = ref.at[pl.ds(0, count)]
        pltpu.make_async_copy(ref, ref, sem).wait()

    def drain_gather():
        pieces, rows = gathered.at[:, :, my_cols], stats.at[:, c]
        sent(pieces, STEPS, g_core)
        sent(rows, Z * X, s_core)
        sent(rows, Z, s_x)

        @pl.when(end)
        def _():
            sent(pieces, 7, g_x)
            sent(pieces, 3, g_z)
            sent(rows, 1, s_z)

        @pl.when(mid)
        def _():
            sent(pieces, 6, g_x)
            sent(pieces, 12, g_z)
            sent(rows, 5, s_z)

    def reduce_step(i, carry):
        @pl.when(i < STEPS)
        def _():
            slot = lax.rem(i, SLOTS)
            pltpu.make_async_copy(dw_buf.at[slot], dw_buf.at[slot], dw_sem.at[slot]).wait()
            part = jnp.dot(hidden[...], dw_buf[slot], preferred_element_type=f32)
            core_out[i] = part[:, :half].astype(bf16)
            core_copy(i).start()
            total[lax.rem(i, 2)] = part[:, half:]

        @pl.when(i < STEPS - SLOTS)
        def _():
            for copy in down(i + SLOTS):
                copy.start()

        @pl.when(i > 0)
        def _():
            with jax.named_scope("finish"):
                finish(i - 1)

        @pl.when(i == STEPS - 2)
        def _():
            drain_gather()

        return carry

    with jax.named_scope("reduce"):
        lax.fori_loop(0, STEPS + 1, reduce_step, 0)

    sent(core_out, STEPS, core_send)
    sent(z_out, (Z - 1) * H, z_send)

    @pl.when(end)
    def _():
        sent(x_out, 7, x_send)
        sent(e_out, 1, e_send)

    @pl.when(mid)
    def _():
        sent(x_out, 6, x_send)
        sent(e_out, 2, e_send)


def fused(activations, norm_gain, gate_weight, up_weight, down_weight):
    tokens, feat = activations.shape
    wide = gate_weight.shape[1]
    n, half = 2 * Z * X, feat // H
    bf16, f32 = jnp.bfloat16, jnp.float32
    anywhere = pl.BlockSpec(memory_space=pl.ANY)
    vmem = pl.BlockSpec(memory_space=pltpu.VMEM)
    dma = pltpu.SemaphoreType.DMA
    return pl.pallas_call(
        kernel,
        out_shape=pltpu.VMEM((tokens, feat), bf16),
        in_specs=[anywhere, vmem, anywhere, anywhere, anywhere],
        out_specs=vmem,
        scratch_shapes=[
            pltpu.VMEM((tokens, feat), bf16),
            pltpu.VMEM((STEPS, tokens, 2 * half), bf16),
            pltpu.VMEM((Z * X, 2, 8, 128), f32),
            pltpu.VMEM((tokens, 128), f32),
            pltpu.VMEM((tokens, 128), f32),
            pltpu.VMEM((SLOTS, 2, 2 * half, wide), bf16),
            pltpu.VMEM((2, tokens, wide), f32),
            pltpu.VMEM((tokens, wide), bf16),
            pltpu.VMEM((SLOTS, wide, 2 * half), bf16),
            pltpu.VMEM((STEPS, tokens, half), bf16),
            pltpu.VMEM((STEPS, tokens, half), bf16),
            pltpu.VMEM((Z * H, tokens, half), bf16),
            pltpu.VMEM((Z * H, tokens, half), bf16),
            pltpu.VMEM((Z * H, tokens, half), bf16),
            pltpu.VMEM((2, Z * H, tokens, half), bf16),
            pltpu.VMEM((2, tokens, half), bf16),
            pltpu.VMEM((2, tokens, half), bf16),
            pltpu.VMEM((2, tokens, half), f32),
            dma,
            dma((SLOTS,)),
            dma((SLOTS,)),
            dma((Z * X,)),
            dma,
            dma,
            dma,
            dma,
            dma((STEPS, 2)),
            dma,
            dma,
            dma,
            dma,
            dma((STEPS,)),
            dma,
            dma((Z * H,)),
            dma,
            dma((2, Z * H)),
            dma,
            dma((2,)),
        ],
        compiler_params=pltpu.CompilerParams(
            collective_id=0, has_side_effects=True, vmem_limit_bytes=62 * 2**20
        ),
    )(activations, norm_gain.reshape(feat // 128, 128), gate_weight, up_weight, down_weight)


def solution(mesh):
    in_specs = (P("groups", "row"), P("row"), P(None, "row"), P(None, "row"), P("row", None))
    out_specs = P("groups", "row")
    n = mesh.shape["row"]

    def per_device(activations, norm_gain, gate_weight, up_weight, down_weight):
        tokens, feat = activations.shape
        fits = (
            n == 2 * Z * X
            and tokens % 128 == 0
            and tokens // 128 <= 8
            and feat % (128 * H) == 0
            and gate_weight.shape[1] % COLS == 0
        )
        body = fused if fits else plain
        return body(activations, norm_gain, gate_weight, up_weight, down_weight)

    return jax.shard_map(
        per_device, mesh=mesh, in_specs=in_specs, out_specs=out_specs, check_vma=False
    )
```

```python
import jax
import jax.numpy as jnp
from jax import lax
from jax.experimental import pallas as pl
from jax.experimental.pallas import tpu as pltpu
from jax.sharding import PartitionSpec as P

D = 8192
Z, X, H = 4, 2, 2
STEPS = Z * X * H
SLOTS = 4
COLS = 256
MESH = pl.DeviceIdType.MESH


GATHER_END = (0, 1, 4, 2, 5, 3, 8, 6, 9, 7, 12, 10, 13, 11, 14, 15)
GATHER_MID = (4, 5, 8, 0, 6, 9, 1, 12, 7, 13, 2, 3, 15, 10, 11, 14)
LATE, LATE_AT = 12, 10
INNER_END, INNER_MID, OUTER_MID = 5, 8, 12
REDUCE_END = (14, 15, 10, 13, 11, 6, 12, 7, 2, 8, 3, 9, 4, 5, 0, 1)
REDUCE_MID = (14, 3, 11, 15, 2, 10, 6, 7, 13, 12, 1, 8, 0, 9, 4, 5)


def plain(activations, norm_gain, gate_weight, up_weight, down_weight):
    float_rows = activations.astype(jnp.float32)
    square_sums = lax.psum(jnp.sum(float_rows * float_rows, axis=1), "row")
    inv_scale = lax.rsqrt(square_sums / D + 1e-05)
    normed = (float_rows * inv_scale[:, None] * norm_gain.astype(jnp.float32)[None, :]).astype(
        jnp.bfloat16
    )
    shard_rows = lax.all_gather(normed, "row", axis=1, tiled=True)
    gate_proj = jnp.dot(shard_rows, gate_weight, preferred_element_type=jnp.float32)
    up_proj = jnp.dot(shard_rows, up_weight, preferred_element_type=jnp.float32)
    hidden = (jax.nn.silu(gate_proj) * up_proj).astype(jnp.bfloat16)
    reduced = lax.psum_scatter(
        lax.dot_general(
            down_weight, hidden, (((0,), (1,)), ((), ())), preferred_element_type=jnp.float32
        ),
        "row",
        scatter_dimension=0,
        tiled=True,
    )
    return reduced.T.astype(jnp.bfloat16)


def kernel(
    act, gain, gate_w, up_w, down_w, out,
    act_buf, gathered, stats, squares, inv, w_buf, acc, hidden, dw_buf,
    core_out, core_in, x_out, x_in, z_out, z_in, e_out, e_in, total,
    act_sem, w_sem, dw_sem, s_recv, s_partner, s_core, s_x, s_z,
    g_recv, g_z, g_x, g_core,
    core_send, core_recv, x_send, x_recv, z_send, z_recv, e_send, e_recv,
):
    n = 2 * Z * X
    bf16, f32 = jnp.bfloat16, jnp.float32
    me = lax.axis_index("row")
    c = lax.rem(me, 2)
    x = lax.rem(me // 2, X)
    z = me // (2 * X)
    tokens, wide = hidden.shape
    feat = act_buf.shape[1]
    half = feat // H
    end = (z == 0) | (z == Z - 1)
    mid = jnp.logical_not(end)
    low = z < Z // 2
    partner = me + 1 - 2 * c
    across = me + 2 - 4 * x
    above = jnp.minimum(me + 2 * X, n - 1)
    below = jnp.maximum(me - 2 * X, 0)
    inner = jnp.where(low, above, below)
    outer = jnp.where(low, below, above)
    my_cols = pl.ds(pl.multiple_of(c * half, half), half)

    def remote(src, dst, send, recv, target):
        return pltpu.make_async_remote_copy(
            src_ref=src, dst_ref=dst, send_sem=send, recv_sem=recv,
            device_id={"row": target}, device_id_type=MESH,
        )

    def pick(table, index):
        value = jnp.int32(table[0])
        for at in range(1, len(table)):
            value = jnp.where(index == at, jnp.int32(table[at]), value)
        return value

    def gather_code(s):
        return jnp.where(end, pick(GATHER_END, s), pick(GATHER_MID, s))

    def reduce_code(i):
        return jnp.where(end, pick(REDUCE_END, i), pick(REDUCE_MID, i))

    def by_z(plane, h):
        return (h == 1) & jnp.where(end, plane == Z - 1, (plane == 0) | (plane == 2))

    def decode(code):
        plane = code // 4
        p = jnp.where(low, plane, Z - 1 - plane)
        other = lax.rem(code // 2, 2)
        h = lax.rem(code, 2)
        chip = p * X + jnp.where(other == 1, 1 - x, x)
        return other == 0, h, plane, p, chip

    def weights(s):
        _, h, _, _, chip = decode(gather_code(s))
        slot = lax.rem(s, SLOTS)
        copies = []
        for i, w in enumerate((gate_w, up_w)):
            for core in range(2):
                start = (chip * 2 + core) * feat + h * half
                rows = pl.ds(pl.multiple_of(start, half), half)
                copies.append(
                    pltpu.make_async_copy(
                        w.at[rows],
                        w_buf.at[slot, i, pl.ds(core * half, half)],
                        w_sem.at[slot],
                    )
                )
        return copies

    def down(i):
        _, h, _, _, chip = decode(reduce_code(i))
        copies = []
        for mine in range(2):
            core = c if mine else 1 - c
            start = (chip * 2 + core) * feat + h * half
            cols = pl.ds(pl.multiple_of(start, half), half)
            slot = jnp.where(i < 2, mine, lax.rem(i, SLOTS))
            place = pl.ds(pl.multiple_of(jnp.where(i < 2, i, mine) * half, half), half)
            copies.append(
                pltpu.make_async_copy(
                    down_w.at[:, cols], dw_buf.at[slot, :, place], dw_sem.at[slot]
                )
            )
        return copies

    own = pltpu.make_async_copy(act, act_buf, act_sem)
    own.start()
    for copy in weights(jnp.int32(0)):
        copy.start()

    barrier = pltpu.get_barrier_semaphore()

    def greet(target):
        pl.semaphore_signal(barrier, inc=1, device_id={"row": target}, device_id_type=MESH)

    greet(partner)
    greet(across)

    @pl.when(z < Z - 1)
    def _():
        greet(above)

    @pl.when(z > 0)
    def _():
        greet(below)

    blocks = tokens // 128
    mine_at = (z * X + x) * H
    gains = gain[...].astype(f32)
    with jax.named_scope("own_wait"):
        own.wait()
    for s in range(1, SLOTS):
        for copy in weights(jnp.int32(s)):
            copy.start()
    for h in range(H):
        for j in range(half // 128):
            at = h * (half // 128) + j
            part = act_buf[:, at * 128 : (at + 1) * 128].astype(f32) * gains[at : at + 1, :]
            cols = pl.ds(pl.multiple_of(c * half + j * 128, 128), 128)
            gathered[mine_at + h, :, cols] = part.astype(bf16)
    with jax.named_scope("barrier_wait"):
        pl.semaphore_wait(barrier, jnp.where(end, 3, 4))

    def pass_core(at):
        ref = gathered.at[at, :, my_cols]
        return remote(ref, ref, g_core, g_recv.at[at, c], partner)

    def passed(chip, h, send, target):
        ref, recv = gathered.at[chip * H + h, :, my_cols], g_recv.at[chip * H + h, c]
        return remote(ref, ref, send, recv, target)

    def pass_x(chip, h):
        return passed(chip, h, g_x, across)

    def pass_up(chip, h):
        return passed(chip, h, g_z, above)

    def pass_down(chip, h):
        return passed(chip, h, g_z, below)

    def tell(chip, send, recv, target):
        ref = stats.at[chip, c]
        return remote(ref, ref, send, recv, target)

    def tell_on(in_line, p, chip):
        tell(chip, s_core, s_partner, partner).start()

        @pl.when(in_line)
        def _():
            tell(chip, s_x, s_recv.at[chip], across).start()

        @pl.when(in_line & (p <= z) & (z < Z - 1))
        def _():
            tell(chip, s_z, s_recv.at[chip], above).start()

        @pl.when(in_line & (p >= z) & (z > 0))
        def _():
            tell(chip, s_z, s_recv.at[chip], below).start()

    def extra(to_inner):
        plane = jnp.where(end, 0, 1) if to_inner else jnp.int32(Z - 1)
        p = jnp.where(low, plane, Z - 1 - plane)
        at = (p * X + 1 - x) * H + 1
        ref, recv = gathered.at[at, :, my_cols], g_recv.at[at, c]
        return remote(ref, ref, g_z, recv, inner if to_inner else outer)

    def arrived(s, core):
        _, h, _, _, chip = decode(gather_code(s))
        at = chip * H + h
        cols = pl.ds(pl.multiple_of(core * half, half), half)
        ref = gathered.at[at, :, cols]
        pltpu.make_async_copy(ref, ref, g_recv.at[at, core]).wait()

    def forward(s):
        in_line, h, plane, p, chip = decode(gather_code(s))
        pass_core(chip * H + h).start()
        late = mid & (gather_code(s) == LATE)

        @pl.when(in_line & jnp.logical_not(by_z(plane, h) | late))
        def _():
            pass_x(chip, h).start()

        @pl.when(in_line & (p <= z) & (z < Z - 1))
        def _():
            pass_up(chip, h).start()

        @pl.when(in_line & (p >= z) & (z > 0))
        def _():
            pass_down(chip, h).start()

        @pl.when(mid & (s == LATE_AT))
        def _():
            _, late_h, _, _, late_chip = decode(jnp.int32(LATE))
            pass_x(late_chip, late_h).start()

        @pl.when((h == 1) & (s >= H))
        def _():
            ref = stats.at[chip, c]
            pltpu.make_async_copy(ref, ref, s_recv.at[chip]).wait()
            tell_on(in_line, p, chip)

        @pl.when(s == jnp.where(end, INNER_END, INNER_MID))
        def _():
            extra(1).start()

        @pl.when(mid & (s == OUTER_MID))
        def _():
            extra(0).start()

    for h in range(H):
        forward(jnp.int32(h))

    rows = act_buf[...].astype(f32)
    sums = jnp.sum(rows * rows, axis=1, keepdims=True)
    squares[...] = jnp.broadcast_to(sums, (tokens, 128))
    for b in range(blocks):
        stats[me // 2, c, b : b + 1, :] = squares[b * 128 : (b + 1) * 128, :].T[0:1, :]

    tell_on(True, z, z * X + x)
    acc[...] = jnp.zeros_like(acc)

    def gather_step(s, carry):
        _, h, _, _, chip = decode(gather_code(s))
        slot = lax.rem(s, SLOTS)
        at = chip * H + h
        fresh = (s == H) | (end & (s > H) & (lax.rem(s, 2) == 0))

        @pl.when(fresh)
        def _():
            with jax.named_scope("link_wait0"):
                arrived(s, c)
            forward(s)

        @pl.when(fresh | (mid & (s > H)))
        def _():
            with jax.named_scope("link_wait1"):
                arrived(s + 1, c)
            forward(s + 1)

        with jax.named_scope("weight_wait"):
            pltpu.make_async_copy(w_buf.at[slot], w_buf.at[slot], w_sem.at[slot]).wait()

        def lane(core):
            cols = pl.ds(pl.multiple_of(core * half, half), half)
            for i in range(2):
                acc[i] += jnp.dot(
                    gathered[at, :, cols], w_buf[slot, i, cols, :], preferred_element_type=f32
                )

        @pl.when(fresh)
        def _():
            lane(c)
            with jax.named_scope("partner_wait0"):
                arrived(s, 1 - c)
            lane(1 - c)

        @pl.when(jnp.logical_not(fresh))
        def _():
            with jax.named_scope("partner_wait"):
                arrived(s, 1 - c)
            for i in range(2):
                acc[i] += jnp.dot(gathered[at], w_buf[slot, i], preferred_element_type=f32)

        @pl.when(s < STEPS - SLOTS)
        def _():
            for copy in weights(s + SLOTS):
                copy.start()

        @pl.when((s >= STEPS // 2) & (s < STEPS // 2 + SLOTS))
        def _():
            for copy in down(s - STEPS // 2):
                copy.start()

        return carry

    with jax.named_scope("gather"):
        lax.fori_loop(0, STEPS - 1, gather_step, 0)

    theirs = stats.at[:, 1 - c]
    pltpu.make_async_copy(theirs, theirs, s_partner).wait()
    sums = stats[0, 0]
    for origin in range(1, n):
        sums = sums + stats[origin // 2, origin % 2]
    scale = lax.rsqrt(sums / (n * feat) + 1e-05)
    for b in range(blocks):
        inv[b * 128 : (b + 1) * 128, :] = jnp.broadcast_to(scale[b : b + 1, :], (128, 128)).T

    with jax.named_scope("activation"):
        last = STEPS - 1
        _, h, _, _, chip = decode(gather_code(last))
        slot, at = last % SLOTS, chip * H + h
        pltpu.make_async_copy(w_buf.at[slot], w_buf.at[slot], w_sem.at[slot]).wait()
        arrived(last, 1 - c)
        for t in range(wide // COLS):
            cols = slice(t * COLS, (t + 1) * COLS)
            gate, up = (
                acc[i, :, cols]
                + jnp.dot(gathered[at], w_buf[slot, i, :, cols], preferred_element_type=f32)
                for i in range(2)
            )
            for q in range(0, COLS, 128):
                by_two = 0.5 * (gate[:, q : q + 128] * inv[...])
                value = by_two * (1.0 + jnp.tanh(by_two)) * (up[:, q : q + 128] * inv[...])
                hidden[:, t * COLS + q : t * COLS + q + 128] = value.astype(bf16)

    def core_copy(i):
        return remote(core_out.at[i], core_in.at[i], core_send, core_recv.at[i], partner)

    def x_copy(at):
        return remote(x_out.at[at], x_in.at[at], x_send, x_recv.at[at], across)

    def z_copy(at, side, target):
        return remote(z_out.at[at], z_in.at[side, at], z_send, z_recv.at[side, at], target)

    def e_copy(side, target):
        return remote(e_out.at[side], e_in.at[side], e_send, e_recv.at[side], target)

    def finish(j):
        in_line, h, plane, p, chip = decode(reduce_code(j))
        cross = jnp.logical_not(in_line)
        special = by_z(plane, h)
        at = p * H + h
        slot = lax.rem(j, 2)
        from_inner = cross & (h == 1) & (p == z)
        from_outer = cross & (h == 1) & mid & (plane == Z - 1)
        with jax.named_scope("core_wait"):
            core_copy(j).wait_recv()
        total[slot] += core_in[j].astype(f32)

        @pl.when(in_line & jnp.logical_not(special))
        def _():
            with jax.named_scope("x_wait"):
                x_copy(at).wait_recv()
            total[slot] += x_in[at].astype(f32)

        @pl.when(in_line & (z > 0) & (p >= z))
        def _():
            with jax.named_scope("zb_wait"):
                z_copy(at, 0, above).wait_recv()
            total[slot] += z_in[0, at].astype(f32)

        @pl.when(in_line & (z < Z - 1) & (p <= z))
        def _():
            with jax.named_scope("za_wait"):
                z_copy(at, 1, below).wait_recv()
            total[slot] += z_in[1, at].astype(f32)

        @pl.when(jnp.where(low, from_outer, from_inner))
        def _():
            with jax.named_scope("e_wait"):
                e_copy(0, above).wait_recv()
            total[slot] += e_in[0].astype(f32)

        @pl.when(jnp.where(low, from_inner, from_outer))
        def _():
            with jax.named_scope("e_wait"):
                e_copy(1, below).wait_recv()
            total[slot] += e_in[1].astype(f32)

        @pl.when(in_line & (p == z))
        def _():
            cols = pl.ds(pl.multiple_of(h * half, half), half)
            out[:, cols] = total[slot].astype(bf16)

        @pl.when(in_line & (p != z))
        def _():
            z_out[at] = total[slot].astype(bf16)

        @pl.when(in_line & (p > z))
        def _():
            z_copy(at, 0, above).start()

        @pl.when(in_line & (p < z))
        def _():
            z_copy(at, 1, below).start()

        @pl.when(cross & jnp.logical_not(special))
        def _():
            x_out[at] = total[slot].astype(bf16)
            x_copy(at).start()

        @pl.when(cross & special & (p > z))
        def _():
            e_out[0] = total[slot].astype(bf16)
            e_copy(0, above).start()

        @pl.when(cross & special & (p < z))
        def _():
            e_out[1] = total[slot].astype(bf16)
            e_copy(1, below).start()

    def sent(ref, count, sem):
        ref = ref.at[pl.ds(0, count)]
        pltpu.make_async_copy(ref, ref, sem).wait()

    def drain_gather():
        pieces, rows = gathered.at[:, :, my_cols], stats.at[:, c]
        sent(pieces, STEPS, g_core)
        sent(rows, Z * X, s_core)
        sent(rows, Z, s_x)

        @pl.when(end)
        def _():
            sent(pieces, 7, g_x)
            sent(pieces, 3, g_z)
            sent(rows, 1, s_z)

        @pl.when(mid)
        def _():
            sent(pieces, 6, g_x)
            sent(pieces, 12, g_z)
            sent(rows, 5, s_z)

    def down_dot(slot):
        pltpu.make_async_copy(dw_buf.at[slot], dw_buf.at[slot], dw_sem.at[slot]).wait()
        return jnp.dot(hidden[...], dw_buf[slot], preferred_element_type=f32)

    def reduce_step(k, carry):
        i = jnp.where(k < 2, k, k - 1)

        @pl.when(k == 0)
        def _():
            part = down_dot(0)
            for one in range(2):
                core_out[one] = part[:, one * half : (one + 1) * half].astype(bf16)
                core_copy(one).start()

        @pl.when(k == 1)
        def _():
            part = down_dot(1)
            for one in range(2):
                total[one] = part[:, one * half : (one + 1) * half]

        @pl.when((k > 2) & (i < STEPS))
        def _():
            part = down_dot(lax.rem(i, SLOTS))
            core_out[i] = part[:, :half].astype(bf16)
            core_copy(i).start()
            total[lax.rem(i, 2)] = part[:, half:]

        @pl.when((k != 2) & (i < STEPS - SLOTS))
        def _():
            for copy in down(i + SLOTS):
                copy.start()

        @pl.when((k == 1) | (k == 2) | (k > 3))
        def _():
            with jax.named_scope("finish"):
                finish(jnp.where(k < 3, k - 1, k - 2))

        @pl.when(k == STEPS - 2)
        def _():
            drain_gather()

        return carry

    with jax.named_scope("reduce"):
        lax.fori_loop(0, STEPS + 2, reduce_step, 0)

    sent(core_out, STEPS, core_send)
    sent(z_out, (Z - 1) * H, z_send)

    @pl.when(end)
    def _():
        sent(x_out, 7, x_send)
        sent(e_out, 1, e_send)

    @pl.when(mid)
    def _():
        sent(x_out, 6, x_send)
        sent(e_out, 2, e_send)


def fused(activations, norm_gain, gate_weight, up_weight, down_weight):
    tokens, feat = activations.shape
    wide = gate_weight.shape[1]
    n, half = 2 * Z * X, feat // H
    bf16, f32 = jnp.bfloat16, jnp.float32
    anywhere = pl.BlockSpec(memory_space=pl.ANY)
    vmem = pl.BlockSpec(memory_space=pltpu.VMEM)
    dma = pltpu.SemaphoreType.DMA
    return pl.pallas_call(
        kernel,
        out_shape=pltpu.VMEM((tokens, feat), bf16),
        in_specs=[anywhere, vmem, anywhere, anywhere, anywhere],
        out_specs=vmem,
        scratch_shapes=[
            pltpu.VMEM((tokens, feat), bf16),
            pltpu.VMEM((STEPS, tokens, 2 * half), bf16),
            pltpu.VMEM((Z * X, 2, 8, 128), f32),
            pltpu.VMEM((tokens, 128), f32),
            pltpu.VMEM((tokens, 128), f32),
            pltpu.VMEM((SLOTS, 2, 2 * half, wide), bf16),
            pltpu.VMEM((2, tokens, wide), f32),
            pltpu.VMEM((tokens, wide), bf16),
            pltpu.VMEM((SLOTS, wide, 2 * half), bf16),
            pltpu.VMEM((STEPS, tokens, half), bf16),
            pltpu.VMEM((STEPS, tokens, half), bf16),
            pltpu.VMEM((Z * H, tokens, half), bf16),
            pltpu.VMEM((Z * H, tokens, half), bf16),
            pltpu.VMEM((Z * H, tokens, half), bf16),
            pltpu.VMEM((2, Z * H, tokens, half), bf16),
            pltpu.VMEM((2, tokens, half), bf16),
            pltpu.VMEM((2, tokens, half), bf16),
            pltpu.VMEM((2, tokens, half), f32),
            dma,
            dma((SLOTS,)),
            dma((SLOTS,)),
            dma((Z * X,)),
            dma,
            dma,
            dma,
            dma,
            dma((STEPS, 2)),
            dma,
            dma,
            dma,
            dma,
            dma((STEPS,)),
            dma,
            dma((Z * H,)),
            dma,
            dma((2, Z * H)),
            dma,
            dma((2,)),
        ],
        compiler_params=pltpu.CompilerParams(
            collective_id=0, has_side_effects=True, vmem_limit_bytes=62 * 2**20
        ),
    )(activations, norm_gain.reshape(feat // 128, 128), gate_weight, up_weight, down_weight)


def solution(mesh):
    in_specs = (P("groups", "row"), P("row"), P(None, "row"), P(None, "row"), P("row", None))
    out_specs = P("groups", "row")
    n = mesh.shape["row"]

    def per_device(activations, norm_gain, gate_weight, up_weight, down_weight):
        tokens, feat = activations.shape
        fits = (
            n == 2 * Z * X
            and tokens % 128 == 0
            and tokens // 128 <= 8
            and feat % (128 * H) == 0
            and gate_weight.shape[1] % COLS == 0
        )
        body = fused if fits else plain
        return body(activations, norm_gain, gate_weight, up_weight, down_weight)

    return jax.shard_map(
        per_device, mesh=mesh, in_specs=in_specs, out_specs=out_specs, check_vma=False
    )
```

```python
import jax
import jax.numpy as jnp
from jax import lax
from jax.experimental import pallas as pl
from jax.experimental.pallas import tpu as pltpu
from jax.sharding import PartitionSpec as P

D = 8192
Z, X, H = 4, 2, 2
STEPS = Z * X * H
SLOTS = 4
COLS = 256
MESH = pl.DeviceIdType.MESH


GATHER_END = (0, 1, 4, 2, 5, 3, 8, 6, 9, 7, 12, 10, 13, 11, 14, 15)
GATHER_MID = (4, 5, 8, 0, 6, 9, 1, 12, 7, 13, 2, 3, 15, 10, 11, 14)
LATE, LATE_AT = 12, 10
INNER_END, INNER_MID, OUTER_MID = 5, 8, 12
REDUCE_END = (14, 15, 10, 13, 11, 6, 12, 7, 2, 8, 3, 9, 4, 5, 0, 1)
REDUCE_MID = (14, 3, 11, 15, 2, 10, 6, 7, 13, 12, 1, 8, 0, 9, 4, 5)


def plain(activations, norm_gain, gate_weight, up_weight, down_weight):
    float_rows = activations.astype(jnp.float32)
    square_sums = lax.psum(jnp.sum(float_rows * float_rows, axis=1), "row")
    inv_scale = lax.rsqrt(square_sums / D + 1e-05)
    normed = (float_rows * inv_scale[:, None] * norm_gain.astype(jnp.float32)[None, :]).astype(
        jnp.bfloat16
    )
    shard_rows = lax.all_gather(normed, "row", axis=1, tiled=True)
    gate_proj = jnp.dot(shard_rows, gate_weight, preferred_element_type=jnp.float32)
    up_proj = jnp.dot(shard_rows, up_weight, preferred_element_type=jnp.float32)
    hidden = (jax.nn.silu(gate_proj) * up_proj).astype(jnp.bfloat16)
    reduced = lax.psum_scatter(
        lax.dot_general(
            down_weight, hidden, (((0,), (1,)), ((), ())), preferred_element_type=jnp.float32
        ),
        "row",
        scatter_dimension=0,
        tiled=True,
    )
    return reduced.T.astype(jnp.bfloat16)


def kernel(
    act, gain, gate_w, up_w, down_w, out,
    act_buf, gathered, stats, squares, inv, w_buf, acc, hidden, dw_buf,
    core_out, core_in, x_out, x_in, z_out, z_in, e_out, e_in, total,
    act_sem, w_sem, dw_sem, s_recv, s_partner, s_core, s_x, s_z,
    g_recv, g_z, g_x, g_core,
    core_send, core_recv, x_send, x_recv, z_send, z_recv, e_send, e_recv, x_half_recv, e_half_recv,
):
    n = 2 * Z * X
    bf16, f32 = jnp.bfloat16, jnp.float32
    me = lax.axis_index("row")
    c = lax.rem(me, 2)
    x = lax.rem(me // 2, X)
    z = me // (2 * X)
    tokens, wide = hidden.shape
    feat = act_buf.shape[1]
    half = feat // H
    short = tokens // 2
    end = (z == 0) | (z == Z - 1)
    mid = jnp.logical_not(end)
    low = z < Z // 2
    partner = me + 1 - 2 * c
    across = me + 2 - 4 * x
    above = jnp.minimum(me + 2 * X, n - 1)
    below = jnp.maximum(me - 2 * X, 0)
    inner = jnp.where(low, above, below)
    outer = jnp.where(low, below, above)
    my_cols = pl.ds(pl.multiple_of(c * half, half), half)

    def remote(src, dst, send, recv, target):
        return pltpu.make_async_remote_copy(
            src_ref=src, dst_ref=dst, send_sem=send, recv_sem=recv,
            device_id={"row": target}, device_id_type=MESH,
        )

    def pick(table, index):
        value = jnp.int32(table[0])
        for at in range(1, len(table)):
            value = jnp.where(index == at, jnp.int32(table[at]), value)
        return value

    def gather_code(s):
        return jnp.where(end, pick(GATHER_END, s), pick(GATHER_MID, s))

    def reduce_code(i):
        return jnp.where(end, pick(REDUCE_END, i), pick(REDUCE_MID, i))

    def by_z(plane, h):
        return (h == 1) & jnp.where(end, plane == Z - 1, (plane == 0) | (plane == 2))

    def decode(code):
        plane = code // 4
        p = jnp.where(low, plane, Z - 1 - plane)
        other = lax.rem(code // 2, 2)
        h = lax.rem(code, 2)
        chip = p * X + jnp.where(other == 1, 1 - x, x)
        return other == 0, h, plane, p, chip

    def weights(s):
        _, h, _, _, chip = decode(gather_code(s))
        slot = lax.rem(s, SLOTS)
        copies = []
        for i, w in enumerate((gate_w, up_w)):
            for core in range(2):
                start = (chip * 2 + core) * feat + h * half
                rows = pl.ds(pl.multiple_of(start, half), half)
                copies.append(
                    pltpu.make_async_copy(
                        w.at[rows],
                        w_buf.at[slot, i, pl.ds(core * half, half)],
                        w_sem.at[slot],
                    )
                )
        return copies

    def down(i):
        _, h, _, _, chip = decode(reduce_code(i))
        copies = []
        for mine in range(2):
            core = c if mine else 1 - c
            start = (chip * 2 + core) * feat + h * half
            cols = pl.ds(pl.multiple_of(start, half), half)
            slot = jnp.where(i < 2, mine, lax.rem(i, SLOTS))
            place = pl.ds(pl.multiple_of(jnp.where(i < 2, i, mine) * half, half), half)
            copies.append(
                pltpu.make_async_copy(
                    down_w.at[:, cols], dw_buf.at[slot, :, place], dw_sem.at[slot]
                )
            )
        return copies

    own = pltpu.make_async_copy(act, act_buf, act_sem)
    own.start()
    for copy in weights(jnp.int32(0)):
        copy.start()

    barrier = pltpu.get_barrier_semaphore()

    def greet(target):
        pl.semaphore_signal(barrier, inc=1, device_id={"row": target}, device_id_type=MESH)

    greet(partner)
    greet(across)

    @pl.when(z < Z - 1)
    def _():
        greet(above)

    @pl.when(z > 0)
    def _():
        greet(below)

    blocks = tokens // 128
    mine_at = (z * X + x) * H
    gains = gain[...].astype(f32)
    with jax.named_scope("own_wait"):
        own.wait()
    for s in range(1, SLOTS):
        for copy in weights(jnp.int32(s)):
            copy.start()
    for h in range(H):
        for j in range(half // 128):
            at = h * (half // 128) + j
            part = act_buf[:, at * 128 : (at + 1) * 128].astype(f32) * gains[at : at + 1, :]
            cols = pl.ds(pl.multiple_of(c * half + j * 128, 128), 128)
            gathered[mine_at + h, :, cols] = part.astype(bf16)
    with jax.named_scope("barrier_wait"):
        pl.semaphore_wait(barrier, jnp.where(end, 3, 4))

    def pass_core(at):
        ref = gathered.at[at, :, my_cols]
        return remote(ref, ref, g_core, g_recv.at[at, c], partner)

    def passed(chip, h, send, target):
        ref, recv = gathered.at[chip * H + h, :, my_cols], g_recv.at[chip * H + h, c]
        return remote(ref, ref, send, recv, target)

    def pass_x(chip, h):
        return passed(chip, h, g_x, across)

    def pass_up(chip, h):
        return passed(chip, h, g_z, above)

    def pass_down(chip, h):
        return passed(chip, h, g_z, below)

    def tell(chip, send, recv, target):
        ref = stats.at[chip, c]
        return remote(ref, ref, send, recv, target)

    def tell_on(in_line, p, chip):
        tell(chip, s_core, s_partner, partner).start()

        @pl.when(in_line)
        def _():
            tell(chip, s_x, s_recv.at[chip], across).start()

        @pl.when(in_line & (p <= z) & (z < Z - 1))
        def _():
            tell(chip, s_z, s_recv.at[chip], above).start()

        @pl.when(in_line & (p >= z) & (z > 0))
        def _():
            tell(chip, s_z, s_recv.at[chip], below).start()

    def extra(to_inner):
        plane = jnp.where(end, 0, 1) if to_inner else jnp.int32(Z - 1)
        p = jnp.where(low, plane, Z - 1 - plane)
        at = (p * X + 1 - x) * H + 1
        ref, recv = gathered.at[at, :, my_cols], g_recv.at[at, c]
        return remote(ref, ref, g_z, recv, inner if to_inner else outer)

    def arrived(s, core):
        _, h, _, _, chip = decode(gather_code(s))
        at = chip * H + h
        cols = pl.ds(pl.multiple_of(core * half, half), half)
        ref = gathered.at[at, :, cols]
        pltpu.make_async_copy(ref, ref, g_recv.at[at, core]).wait()

    def forward(s):
        in_line, h, plane, p, chip = decode(gather_code(s))
        pass_core(chip * H + h).start()
        late = mid & (gather_code(s) == LATE)

        @pl.when(in_line & jnp.logical_not(by_z(plane, h) | late))
        def _():
            pass_x(chip, h).start()

        @pl.when(in_line & (p <= z) & (z < Z - 1))
        def _():
            pass_up(chip, h).start()

        @pl.when(in_line & (p >= z) & (z > 0))
        def _():
            pass_down(chip, h).start()

        @pl.when(mid & (s == LATE_AT))
        def _():
            _, late_h, _, _, late_chip = decode(jnp.int32(LATE))
            pass_x(late_chip, late_h).start()

        @pl.when((h == 1) & (s >= H))
        def _():
            ref = stats.at[chip, c]
            pltpu.make_async_copy(ref, ref, s_recv.at[chip]).wait()
            tell_on(in_line, p, chip)

        @pl.when(s == jnp.where(end, INNER_END, INNER_MID))
        def _():
            extra(1).start()

        @pl.when(mid & (s == OUTER_MID))
        def _():
            extra(0).start()

    for h in range(H):
        forward(jnp.int32(h))

    rows = act_buf[...].astype(f32)
    sums = jnp.sum(rows * rows, axis=1, keepdims=True)
    squares[...] = jnp.broadcast_to(sums, (tokens, 128))
    for b in range(blocks):
        stats[me // 2, c, b : b + 1, :] = squares[b * 128 : (b + 1) * 128, :].T[0:1, :]

    tell_on(True, z, z * X + x)
    acc[...] = jnp.zeros_like(acc)

    def gather_step(s, carry):
        _, h, _, _, chip = decode(gather_code(s))
        slot = lax.rem(s, SLOTS)
        at = chip * H + h
        fresh = (s == H) | (end & (s > H) & (lax.rem(s, 2) == 0))

        @pl.when(fresh)
        def _():
            with jax.named_scope("link_wait0"):
                arrived(s, c)
            forward(s)

        @pl.when(fresh | (mid & (s > H)))
        def _():
            with jax.named_scope("link_wait1"):
                arrived(s + 1, c)
            forward(s + 1)

        with jax.named_scope("weight_wait"):
            pltpu.make_async_copy(w_buf.at[slot], w_buf.at[slot], w_sem.at[slot]).wait()

        def lane(core):
            cols = pl.ds(pl.multiple_of(core * half, half), half)
            for i in range(2):
                acc[i] += jnp.dot(
                    gathered[at, :, cols], w_buf[slot, i, cols, :], preferred_element_type=f32
                )

        @pl.when(fresh)
        def _():
            lane(c)
            with jax.named_scope("partner_wait0"):
                arrived(s, 1 - c)
            lane(1 - c)

        @pl.when(jnp.logical_not(fresh))
        def _():
            with jax.named_scope("partner_wait"):
                arrived(s, 1 - c)
            for i in range(2):
                acc[i] += jnp.dot(gathered[at], w_buf[slot, i], preferred_element_type=f32)

        @pl.when(s < STEPS - SLOTS)
        def _():
            for copy in weights(s + SLOTS):
                copy.start()

        @pl.when((s >= STEPS // 2) & (s < STEPS // 2 + SLOTS))
        def _():
            for copy in down(s - STEPS // 2):
                copy.start()

        return carry

    with jax.named_scope("gather"):
        lax.fori_loop(0, STEPS - 1, gather_step, 0)

    theirs = stats.at[:, 1 - c]
    pltpu.make_async_copy(theirs, theirs, s_partner).wait()
    sums = stats[0, 0]
    for origin in range(1, n):
        sums = sums + stats[origin // 2, origin % 2]
    scale = lax.rsqrt(sums / (n * feat) + 1e-05)
    for b in range(blocks):
        inv[b * 128 : (b + 1) * 128, :] = jnp.broadcast_to(scale[b : b + 1, :], (128, 128)).T

    def core_copy(i):
        return remote(core_out.at[i], core_in.at[i], core_send, core_recv.at[i], partner)

    def x_copy(at):
        return remote(x_out.at[at], x_in.at[at], x_send, x_recv.at[at], across)

    def z_copy(at, side, target):
        return remote(z_out.at[at], z_in.at[side, at], z_send, z_recv.at[side, at], target)

    def e_copy(side, target):
        return remote(e_out.at[side], e_in.at[side], e_send, e_recv.at[side], target)

    def some_rows(r):
        return pl.ds(pl.multiple_of(r * short, short), short)

    def first_core(r):
        return remote(
            core_out.at[pl.ds(0, 2), some_rows(r)], core_in.at[pl.ds(0, 2), some_rows(r)],
            core_send, core_recv.at[r], partner,
        )

    def x_half(r):
        far = jnp.where(low, Z - 1, 0) * H
        return remote(
            x_out.at[far, some_rows(r)], x_in.at[far, some_rows(r)], x_send, x_half_recv.at[r],
            across,
        )

    def e_half(r, side, target):
        return remote(
            e_out.at[side, some_rows(r)], e_in.at[side, some_rows(r)], e_send, e_half_recv.at[r],
            target,
        )

    def boundary(r, carry):
        rows = pl.ds(pl.multiple_of(r * short, short), short)
        last = STEPS - 1
        _, h, _, _, chip = decode(gather_code(last))
        slot, at = last % SLOTS, chip * H + h
        for t in range(wide // COLS):
            cols = slice(t * COLS, (t + 1) * COLS)
            gate, up = (
                acc[i, rows, cols]
                + jnp.dot(
                    gathered[at, rows, :], w_buf[slot, i, :, cols], preferred_element_type=f32
                )
                for i in range(2)
            )
            for q in range(0, COLS, 128):
                scaling = inv[rows, :]
                by_two = 0.5 * (gate[:, q : q + 128] * scaling)
                value = by_two * (1.0 + jnp.tanh(by_two)) * (up[:, q : q + 128] * scaling)
                hidden[rows, t * COLS + q : t * COLS + q + 128] = value.astype(bf16)

        @pl.when(r == 0)
        def _():
            for first in range(2):
                pltpu.make_async_copy(dw_buf.at[first], dw_buf.at[first], dw_sem.at[first]).wait()

        part = jnp.dot(hidden[rows, :], dw_buf[0], preferred_element_type=f32)
        for one in range(2):
            core_out[one, rows, :] = part[:, one * half : (one + 1) * half].astype(bf16)
        first_core(r).start()
        part = jnp.dot(hidden[rows, :], dw_buf[1], preferred_element_type=f32)
        with jax.named_scope("first_wait"):
            first_core(r).wait_recv()
        far, up_side = jnp.where(low, Z - 1, 0) * H, jnp.where(end, low, jnp.logical_not(low))
        side = jnp.where(up_side, 0, 1)
        x_out[far, rows, :] = (part[:, :half] + core_in[0, rows, :].astype(f32)).astype(bf16)
        x_half(r).start()
        e_out[side, rows, :] = (part[:, half:] + core_in[1, rows, :].astype(f32)).astype(bf16)

        @pl.when(up_side)
        def _():
            e_half(r, 0, above).start()

        @pl.when(jnp.logical_not(up_side))
        def _():
            e_half(r, 1, below).start()

        return carry

    def finish(j):
        in_line, h, plane, p, chip = decode(reduce_code(j))
        cross = jnp.logical_not(in_line)
        special = by_z(plane, h)
        at = p * H + h
        slot = lax.rem(j, 2)
        from_inner = cross & (h == 1) & (p == z)
        from_outer = cross & (h == 1) & mid & (plane == Z - 1)
        with jax.named_scope("core_wait"):
            core_copy(j).wait_recv()
        total[slot] += core_in[j].astype(f32)

        @pl.when(in_line & jnp.logical_not(special))
        def _():
            far = (plane == Z - 1) & (h == 0)

            @pl.when(far)
            def _():
                for r in range(2):
                    x_half(r).wait_recv()

            @pl.when(jnp.logical_not(far))
            def _():
                x_copy(at).wait_recv()

            total[slot] += x_in[at].astype(f32)

        @pl.when(in_line & (z > 0) & (p >= z))
        def _():
            with jax.named_scope("zb_wait"):
                z_copy(at, 0, above).wait_recv()
            total[slot] += z_in[0, at].astype(f32)

        @pl.when(in_line & (z < Z - 1) & (p <= z))
        def _():
            with jax.named_scope("za_wait"):
                z_copy(at, 1, below).wait_recv()
            total[slot] += z_in[1, at].astype(f32)

        @pl.when(jnp.where(low, from_outer, from_inner))
        def _():
            @pl.when(end | from_outer)
            def _():
                for r in range(2):
                    e_half(r, 0, above).wait_recv()

            @pl.when(jnp.logical_not(end | from_outer))
            def _():
                e_copy(0, above).wait_recv()

            total[slot] += e_in[0].astype(f32)

        @pl.when(jnp.where(low, from_inner, from_outer))
        def _():
            @pl.when(end | from_outer)
            def _():
                for r in range(2):
                    e_half(r, 1, below).wait_recv()

            @pl.when(jnp.logical_not(end | from_outer))
            def _():
                e_copy(1, below).wait_recv()

            total[slot] += e_in[1].astype(f32)

        @pl.when(in_line & (p == z))
        def _():
            cols = pl.ds(pl.multiple_of(h * half, half), half)
            out[:, cols] = total[slot].astype(bf16)

        @pl.when(in_line & (p != z))
        def _():
            z_out[at] = total[slot].astype(bf16)

        @pl.when(in_line & (p > z))
        def _():
            z_copy(at, 0, above).start()

        @pl.when(in_line & (p < z))
        def _():
            z_copy(at, 1, below).start()

        @pl.when(cross & jnp.logical_not(special))
        def _():
            x_out[at] = total[slot].astype(bf16)
            x_copy(at).start()

        @pl.when(cross & special & (p > z))
        def _():
            e_out[0] = total[slot].astype(bf16)
            e_copy(0, above).start()

        @pl.when(cross & special & (p < z))
        def _():
            e_out[1] = total[slot].astype(bf16)
            e_copy(1, below).start()

    def sent(ref, count, sem):
        ref = ref.at[pl.ds(0, count)]
        pltpu.make_async_copy(ref, ref, sem).wait()

    def drain_gather():
        pieces, rows = gathered.at[:, :, my_cols], stats.at[:, c]
        sent(pieces, STEPS, g_core)
        sent(rows, Z * X, s_core)
        sent(rows, Z, s_x)

        @pl.when(end)
        def _():
            sent(pieces, 7, g_x)
            sent(pieces, 3, g_z)
            sent(rows, 1, s_z)

        @pl.when(mid)
        def _():
            sent(pieces, 6, g_x)
            sent(pieces, 12, g_z)
            sent(rows, 5, s_z)

    def down_dot(slot):
        pltpu.make_async_copy(dw_buf.at[slot], dw_buf.at[slot], dw_sem.at[slot]).wait()
        return jnp.dot(hidden[...], dw_buf[slot], preferred_element_type=f32)

    def reduce_step(i, carry):
        @pl.when(i < STEPS)
        def _():
            part = down_dot(lax.rem(i, SLOTS))
            core_out[i] = part[:, :half].astype(bf16)
            core_copy(i).start()
            total[lax.rem(i, 2)] = part[:, half:]

        @pl.when(i < STEPS - SLOTS)
        def _():
            for copy in down(i + SLOTS):
                copy.start()

        @pl.when(i > 2)
        def _():
            with jax.named_scope("finish"):
                finish(i - 1)

        @pl.when(i == STEPS - 2)
        def _():
            drain_gather()

        return carry

    pltpu.make_async_copy(
        w_buf.at[(STEPS - 1) % SLOTS], w_buf.at[(STEPS - 1) % SLOTS], w_sem.at[(STEPS - 1) % SLOTS]
    ).wait()
    arrived(STEPS - 1, 1 - c)
    with jax.named_scope("boundary"):
        lax.fori_loop(0, 2, boundary, 0)
    for i in range(2):
        for copy in down(i + SLOTS):
            copy.start()
    with jax.named_scope("reduce"):
        lax.fori_loop(2, STEPS + 1, reduce_step, 0)

    sent(core_out, STEPS, core_send)
    sent(z_out, (Z - 1) * H, z_send)

    @pl.when(end)
    def _():
        sent(x_out, 7, x_send)
        sent(e_out, 1, e_send)

    @pl.when(mid)
    def _():
        sent(x_out, 6, x_send)
        sent(e_out, 2, e_send)


def fused(activations, norm_gain, gate_weight, up_weight, down_weight):
    tokens, feat = activations.shape
    wide = gate_weight.shape[1]
    n, half = 2 * Z * X, feat // H
    bf16, f32 = jnp.bfloat16, jnp.float32
    anywhere = pl.BlockSpec(memory_space=pl.ANY)
    vmem = pl.BlockSpec(memory_space=pltpu.VMEM)
    dma = pltpu.SemaphoreType.DMA
    return pl.pallas_call(
        kernel,
        out_shape=pltpu.VMEM((tokens, feat), bf16),
        in_specs=[anywhere, vmem, anywhere, anywhere, anywhere],
        out_specs=vmem,
        scratch_shapes=[
            pltpu.VMEM((tokens, feat), bf16),
            pltpu.VMEM((STEPS, tokens, 2 * half), bf16),
            pltpu.VMEM((Z * X, 2, 8, 128), f32),
            pltpu.VMEM((tokens, 128), f32),
            pltpu.VMEM((tokens, 128), f32),
            pltpu.VMEM((SLOTS, 2, 2 * half, wide), bf16),
            pltpu.VMEM((2, tokens, wide), f32),
            pltpu.VMEM((tokens, wide), bf16),
            pltpu.VMEM((SLOTS, wide, 2 * half), bf16),
            pltpu.VMEM((STEPS, tokens, half), bf16),
            pltpu.VMEM((STEPS, tokens, half), bf16),
            pltpu.VMEM((Z * H, tokens, half), bf16),
            pltpu.VMEM((Z * H, tokens, half), bf16),
            pltpu.VMEM((Z * H, tokens, half), bf16),
            pltpu.VMEM((2, Z * H, tokens, half), bf16),
            pltpu.VMEM((2, tokens, half), bf16),
            pltpu.VMEM((2, tokens, half), bf16),
            pltpu.VMEM((2, tokens, half), f32),
            dma,
            dma((SLOTS,)),
            dma((SLOTS,)),
            dma((Z * X,)),
            dma,
            dma,
            dma,
            dma,
            dma((STEPS, 2)),
            dma,
            dma,
            dma,
            dma,
            dma((STEPS,)),
            dma,
            dma((Z * H,)),
            dma,
            dma((2, Z * H)),
            dma,
            dma((2,)),
            dma((2,)),
            dma((2,)),
        ],
        compiler_params=pltpu.CompilerParams(
            collective_id=0, has_side_effects=True, vmem_limit_bytes=62 * 2**20
        ),
    )(activations, norm_gain.reshape(feat // 128, 128), gate_weight, up_weight, down_weight)


def solution(mesh):
    in_specs = (P("groups", "row"), P("row"), P(None, "row"), P(None, "row"), P("row", None))
    out_specs = P("groups", "row")
    n = mesh.shape["row"]

    def per_device(activations, norm_gain, gate_weight, up_weight, down_weight):
        tokens, feat = activations.shape
        fits = (
            n == 2 * Z * X
            and tokens % 128 == 0
            and tokens // 128 <= 8
            and feat % (128 * H) == 0
            and gate_weight.shape[1] % COLS == 0
        )
        body = fused if fits else plain
        return body(activations, norm_gain, gate_weight, up_weight, down_weight)

    return jax.shard_map(
        per_device, mesh=mesh, in_specs=in_specs, out_specs=out_specs, check_vma=False
    )
```

```python
import jax
import jax.numpy as jnp
from jax import lax
from jax.experimental import pallas as pl
from jax.experimental.pallas import tpu as pltpu
from jax.sharding import PartitionSpec as P

D = 8192
Z, X, H = 4, 2, 2
STEPS = Z * X * H
SLOTS = 4
COLS = 256
MESH = pl.DeviceIdType.MESH


GATHER_END = (0, 1, 4, 2, 5, 3, 8, 6, 9, 7, 12, 10, 13, 11, 14, 15)
GATHER_MID = (4, 5, 8, 0, 6, 9, 1, 12, 7, 13, 2, 3, 15, 10, 11, 14)
LATE, LATE_AT = 12, 10
INNER_END, INNER_MID, OUTER_MID = 5, 8, 12
REDUCE_END = (14, 15, 10, 13, 11, 12, 6, 7, 2, 8, 3, 9, 4, 5, 0, 1)
REDUCE_MID = (14, 3, 11, 15, 2, 10, 6, 7, 13, 12, 1, 8, 0, 9, 4, 5)


def plain(activations, norm_gain, gate_weight, up_weight, down_weight):
    float_rows = activations.astype(jnp.float32)
    square_sums = lax.psum(jnp.sum(float_rows * float_rows, axis=1), "row")
    inv_scale = lax.rsqrt(square_sums / D + 1e-05)
    normed = (float_rows * inv_scale[:, None] * norm_gain.astype(jnp.float32)[None, :]).astype(
        jnp.bfloat16
    )
    shard_rows = lax.all_gather(normed, "row", axis=1, tiled=True)
    gate_proj = jnp.dot(shard_rows, gate_weight, preferred_element_type=jnp.float32)
    up_proj = jnp.dot(shard_rows, up_weight, preferred_element_type=jnp.float32)
    hidden = (jax.nn.silu(gate_proj) * up_proj).astype(jnp.bfloat16)
    reduced = lax.psum_scatter(
        lax.dot_general(
            down_weight, hidden, (((0,), (1,)), ((), ())), preferred_element_type=jnp.float32
        ),
        "row",
        scatter_dimension=0,
        tiled=True,
    )
    return reduced.T.astype(jnp.bfloat16)


def kernel(
    act, gain, gate_w, up_w, down_w, out,
    act_buf, gathered, stats, squares, inv, w_buf, acc, hidden, dw_buf,
    core_out, core_in, x_out, x_in, z_out, z_in, e_out, e_in, total,
    act_sem, w_sem, dw_sem, s_recv, s_partner, s_core, s_x, s_z,
    g_recv, g_z, g_x, g_core,
    core_send, core_recv, x_send, x_recv, z_send, z_recv, e_send, e_recv, x_half_recv, e_half_recv,
):
    n = 2 * Z * X
    bf16, f32 = jnp.bfloat16, jnp.float32
    me = lax.axis_index("row")
    c = lax.rem(me, 2)
    x = lax.rem(me // 2, X)
    z = me // (2 * X)
    tokens, wide = hidden.shape
    feat = act_buf.shape[1]
    half = feat // H
    short = tokens // 2
    end = (z == 0) | (z == Z - 1)
    mid = jnp.logical_not(end)
    low = z < Z // 2
    partner = me + 1 - 2 * c
    across = me + 2 - 4 * x
    above = jnp.minimum(me + 2 * X, n - 1)
    below = jnp.maximum(me - 2 * X, 0)
    inner = jnp.where(low, above, below)
    outer = jnp.where(low, below, above)
    my_cols = pl.ds(pl.multiple_of(c * half, half), half)

    def remote(src, dst, send, recv, target):
        return pltpu.make_async_remote_copy(
            src_ref=src, dst_ref=dst, send_sem=send, recv_sem=recv,
            device_id={"row": target}, device_id_type=MESH,
        )

    def pick(table, index):
        value = jnp.int32(table[0])
        for at in range(1, len(table)):
            value = jnp.where(index == at, jnp.int32(table[at]), value)
        return value

    def gather_code(s):
        return jnp.where(end, pick(GATHER_END, s), pick(GATHER_MID, s))

    def reduce_code(i):
        return jnp.where(end, pick(REDUCE_END, i), pick(REDUCE_MID, i))

    def by_z(plane, h):
        return (h == 1) & jnp.where(end, plane == Z - 1, (plane == 0) | (plane == 2))

    def decode(code):
        plane = code // 4
        p = jnp.where(low, plane, Z - 1 - plane)
        other = lax.rem(code // 2, 2)
        h = lax.rem(code, 2)
        chip = p * X + jnp.where(other == 1, 1 - x, x)
        return other == 0, h, plane, p, chip

    def weights(s):
        _, h, _, _, chip = decode(gather_code(s))
        slot = lax.rem(s, SLOTS)
        copies = []
        for i, w in enumerate((gate_w, up_w)):
            for core in range(2):
                start = (chip * 2 + core) * feat + h * half
                rows = pl.ds(pl.multiple_of(start, half), half)
                copies.append(
                    pltpu.make_async_copy(
                        w.at[rows],
                        w_buf.at[slot, i, pl.ds(core * half, half)],
                        w_sem.at[slot],
                    )
                )
        return copies

    def down(i):
        _, h, _, _, chip = decode(reduce_code(i))
        copies = []
        for mine in range(2):
            core = c if mine else 1 - c
            start = (chip * 2 + core) * feat + h * half
            cols = pl.ds(pl.multiple_of(start, half), half)
            slot = jnp.where(i < 2, mine, lax.rem(i, SLOTS))
            place = pl.ds(pl.multiple_of(jnp.where(i < 2, i, mine) * half, half), half)
            copies.append(
                pltpu.make_async_copy(
                    down_w.at[:, cols], dw_buf.at[slot, :, place], dw_sem.at[slot]
                )
            )
        return copies

    own = pltpu.make_async_copy(act, act_buf, act_sem)
    own.start()
    for copy in weights(jnp.int32(0)):
        copy.start()

    barrier = pltpu.get_barrier_semaphore()

    def greet(target):
        pl.semaphore_signal(barrier, inc=1, device_id={"row": target}, device_id_type=MESH)

    greet(partner)
    greet(across)

    @pl.when(z < Z - 1)
    def _():
        greet(above)

    @pl.when(z > 0)
    def _():
        greet(below)

    blocks = tokens // 128
    mine_at = (z * X + x) * H
    gains = gain[...].astype(f32)
    with jax.named_scope("own_wait"):
        own.wait()
    for s in range(1, SLOTS):
        for copy in weights(jnp.int32(s)):
            copy.start()
    for h in range(H):
        for j in range(half // 128):
            at = h * (half // 128) + j
            part = act_buf[:, at * 128 : (at + 1) * 128].astype(f32) * gains[at : at + 1, :]
            cols = pl.ds(pl.multiple_of(c * half + j * 128, 128), 128)
            gathered[mine_at + h, :, cols] = part.astype(bf16)
    with jax.named_scope("barrier_wait"):
        pl.semaphore_wait(barrier, jnp.where(end, 3, 4))

    def pass_core(at):
        ref = gathered.at[at, :, my_cols]
        return remote(ref, ref, g_core, g_recv.at[at, c], partner)

    def passed(chip, h, send, target):
        ref, recv = gathered.at[chip * H + h, :, my_cols], g_recv.at[chip * H + h, c]
        return remote(ref, ref, send, recv, target)

    def pass_x(chip, h):
        return passed(chip, h, g_x, across)

    def pass_up(chip, h):
        return passed(chip, h, g_z, above)

    def pass_down(chip, h):
        return passed(chip, h, g_z, below)

    def tell(chip, send, recv, target):
        ref = stats.at[chip, c]
        return remote(ref, ref, send, recv, target)

    def tell_on(in_line, p, chip):
        tell(chip, s_core, s_partner, partner).start()

        @pl.when(in_line)
        def _():
            tell(chip, s_x, s_recv.at[chip], across).start()

        @pl.when(in_line & (p <= z) & (z < Z - 1))
        def _():
            tell(chip, s_z, s_recv.at[chip], above).start()

        @pl.when(in_line & (p >= z) & (z > 0))
        def _():
            tell(chip, s_z, s_recv.at[chip], below).start()

    def extra(to_inner):
        plane = jnp.where(end, 0, 1) if to_inner else jnp.int32(Z - 1)
        p = jnp.where(low, plane, Z - 1 - plane)
        at = (p * X + 1 - x) * H + 1
        ref, recv = gathered.at[at, :, my_cols], g_recv.at[at, c]
        return remote(ref, ref, g_z, recv, inner if to_inner else outer)

    def arrived(s, core):
        _, h, _, _, chip = decode(gather_code(s))
        at = chip * H + h
        cols = pl.ds(pl.multiple_of(core * half, half), half)
        ref = gathered.at[at, :, cols]
        pltpu.make_async_copy(ref, ref, g_recv.at[at, core]).wait()

    def forward(s):
        in_line, h, plane, p, chip = decode(gather_code(s))
        pass_core(chip * H + h).start()
        late = mid & (gather_code(s) == LATE)

        @pl.when(in_line & jnp.logical_not(by_z(plane, h) | late))
        def _():
            pass_x(chip, h).start()

        @pl.when(in_line & (p <= z) & (z < Z - 1))
        def _():
            pass_up(chip, h).start()

        @pl.when(in_line & (p >= z) & (z > 0))
        def _():
            pass_down(chip, h).start()

        @pl.when(mid & (s == LATE_AT))
        def _():
            _, late_h, _, _, late_chip = decode(jnp.int32(LATE))
            pass_x(late_chip, late_h).start()

        @pl.when((h == 1) & (s >= H))
        def _():
            ref = stats.at[chip, c]
            pltpu.make_async_copy(ref, ref, s_recv.at[chip]).wait()
            tell_on(in_line, p, chip)

        @pl.when(s == jnp.where(end, INNER_END, INNER_MID))
        def _():
            extra(1).start()

        @pl.when(mid & (s == OUTER_MID))
        def _():
            extra(0).start()

    for h in range(H):
        forward(jnp.int32(h))

    rows = act_buf[...].astype(f32)
    sums = jnp.sum(rows * rows, axis=1, keepdims=True)
    squares[...] = jnp.broadcast_to(sums, (tokens, 128))
    for b in range(blocks):
        stats[me // 2, c, b : b + 1, :] = squares[b * 128 : (b + 1) * 128, :].T[0:1, :]

    tell_on(True, z, z * X + x)
    acc[...] = jnp.zeros_like(acc)

    def gather_step(s, carry):
        _, h, _, _, chip = decode(gather_code(s))
        slot = lax.rem(s, SLOTS)
        at = chip * H + h
        fresh = (s == H) | (end & (s > H) & (lax.rem(s, 2) == 0))

        @pl.when(fresh)
        def _():
            with jax.named_scope("link_wait0"):
                arrived(s, c)
            forward(s)

        @pl.when(fresh | (mid & (s > H)))
        def _():
            with jax.named_scope("link_wait1"):
                arrived(s + 1, c)
            forward(s + 1)

        with jax.named_scope("weight_wait"):
            pltpu.make_async_copy(w_buf.at[slot], w_buf.at[slot], w_sem.at[slot]).wait()

        def lane(core):
            cols = pl.ds(pl.multiple_of(core * half, half), half)
            for i in range(2):
                acc[i] += jnp.dot(
                    gathered[at, :, cols], w_buf[slot, i, cols, :], preferred_element_type=f32
                )

        @pl.when(fresh)
        def _():
            lane(c)
            with jax.named_scope("partner_wait0"):
                arrived(s, 1 - c)
            lane(1 - c)

        @pl.when(jnp.logical_not(fresh))
        def _():
            with jax.named_scope("partner_wait"):
                arrived(s, 1 - c)
            for i in range(2):
                acc[i] += jnp.dot(gathered[at], w_buf[slot, i], preferred_element_type=f32)

        @pl.when(s < STEPS - SLOTS)
        def _():
            for copy in weights(s + SLOTS):
                copy.start()

        @pl.when((s >= STEPS // 2) & (s < STEPS // 2 + SLOTS))
        def _():
            for copy in down(s - STEPS // 2):
                copy.start()

        return carry

    with jax.named_scope("gather"):
        lax.fori_loop(0, STEPS - 1, gather_step, 0)

    theirs = stats.at[:, 1 - c]
    pltpu.make_async_copy(theirs, theirs, s_partner).wait()
    sums = stats[0, 0]
    for origin in range(1, n):
        sums = sums + stats[origin // 2, origin % 2]
    scale = lax.rsqrt(sums / (n * feat) + 1e-05)
    for b in range(blocks):
        inv[b * 128 : (b + 1) * 128, :] = jnp.broadcast_to(scale[b : b + 1, :], (128, 128)).T

    def core_copy(i):
        return remote(core_out.at[i], core_in.at[i], core_send, core_recv.at[i], partner)

    def x_copy(at):
        return remote(x_out.at[at], x_in.at[at], x_send, x_recv.at[at], across)

    def z_copy(at, side, target):
        return remote(z_out.at[at], z_in.at[side, at], z_send, z_recv.at[side, at], target)

    def e_copy(side, target):
        return remote(e_out.at[side], e_in.at[side], e_send, e_recv.at[side], target)

    def some_rows(r):
        return pl.ds(pl.multiple_of(r * short, short), short)

    def first_core(r):
        return remote(
            core_out.at[pl.ds(0, 2), some_rows(r)], core_in.at[pl.ds(0, 2), some_rows(r)],
            core_send, core_recv.at[r], partner,
        )

    def x_half(r):
        far = jnp.where(low, Z - 1, 0) * H
        return remote(
            x_out.at[far, some_rows(r)], x_in.at[far, some_rows(r)], x_send, x_half_recv.at[r],
            across,
        )

    def e_half(r, side, target):
        return remote(
            e_out.at[side, some_rows(r)], e_in.at[side, some_rows(r)], e_send, e_half_recv.at[r],
            target,
        )

    def boundary(r, carry):
        rows = pl.ds(pl.multiple_of(r * short, short), short)
        last = STEPS - 1
        _, h, _, _, chip = decode(gather_code(last))
        slot, at = last % SLOTS, chip * H + h
        for t in range(wide // COLS):
            cols = slice(t * COLS, (t + 1) * COLS)
            gate, up = (
                acc[i, rows, cols]
                + jnp.dot(
                    gathered[at, rows, :], w_buf[slot, i, :, cols], preferred_element_type=f32
                )
                for i in range(2)
            )
            for q in range(0, COLS, 128):
                scaling = inv[rows, :]
                by_two = 0.5 * (gate[:, q : q + 128] * scaling)
                value = by_two * (1.0 + jnp.tanh(by_two)) * (up[:, q : q + 128] * scaling)
                hidden[rows, t * COLS + q : t * COLS + q + 128] = value.astype(bf16)

        @pl.when(r == 0)
        def _():
            for first in range(2):
                pltpu.make_async_copy(dw_buf.at[first], dw_buf.at[first], dw_sem.at[first]).wait()

        part = jnp.dot(hidden[rows, :], dw_buf[0], preferred_element_type=f32)
        for one in range(2):
            core_out[one, rows, :] = part[:, one * half : (one + 1) * half].astype(bf16)
        first_core(r).start()
        part = jnp.dot(hidden[rows, :], dw_buf[1], preferred_element_type=f32)
        with jax.named_scope("first_wait"):
            first_core(r).wait_recv()
        far, up_side = jnp.where(low, Z - 1, 0) * H, jnp.where(end, low, jnp.logical_not(low))
        side = jnp.where(up_side, 0, 1)
        x_out[far, rows, :] = (part[:, :half] + core_in[0, rows, :].astype(f32)).astype(bf16)
        x_half(r).start()
        e_out[side, rows, :] = (part[:, half:] + core_in[1, rows, :].astype(f32)).astype(bf16)

        @pl.when(up_side)
        def _():
            e_half(r, 0, above).start()

        @pl.when(jnp.logical_not(up_side))
        def _():
            e_half(r, 1, below).start()

        return carry

    def finish(j):
        in_line, h, plane, p, chip = decode(reduce_code(j))
        cross = jnp.logical_not(in_line)
        special = by_z(plane, h)
        at = p * H + h
        slot = lax.rem(j, 2)
        from_inner = cross & (h == 1) & (p == z)
        from_outer = cross & (h == 1) & mid & (plane == Z - 1)
        with jax.named_scope("core_wait"):
            core_copy(j).wait_recv()
        total[slot] += core_in[j].astype(f32)

        @pl.when(in_line & jnp.logical_not(special))
        def _():
            far = (plane == Z - 1) & (h == 0)

            @pl.when(far)
            def _():
                for r in range(2):
                    x_half(r).wait_recv()

            @pl.when(jnp.logical_not(far))
            def _():
                x_copy(at).wait_recv()

            total[slot] += x_in[at].astype(f32)

        @pl.when(in_line & (z > 0) & (p >= z))
        def _():
            with jax.named_scope("zb_wait"):
                z_copy(at, 0, above).wait_recv()
            total[slot] += z_in[0, at].astype(f32)

        @pl.when(in_line & (z < Z - 1) & (p <= z))
        def _():
            with jax.named_scope("za_wait"):
                z_copy(at, 1, below).wait_recv()
            total[slot] += z_in[1, at].astype(f32)

        @pl.when(jnp.where(low, from_outer, from_inner))
        def _():
            @pl.when(end | from_outer)
            def _():
                for r in range(2):
                    e_half(r, 0, above).wait_recv()

            @pl.when(jnp.logical_not(end | from_outer))
            def _():
                e_copy(0, above).wait_recv()

            total[slot] += e_in[0].astype(f32)

        @pl.when(jnp.where(low, from_inner, from_outer))
        def _():
            @pl.when(end | from_outer)
            def _():
                for r in range(2):
                    e_half(r, 1, below).wait_recv()

            @pl.when(jnp.logical_not(end | from_outer))
            def _():
                e_copy(1, below).wait_recv()

            total[slot] += e_in[1].astype(f32)

        @pl.when(in_line & (p == z))
        def _():
            cols = pl.ds(pl.multiple_of(h * half, half), half)
            out[:, cols] = total[slot].astype(bf16)

        @pl.when(in_line & (p != z))
        def _():
            z_out[at] = total[slot].astype(bf16)

        @pl.when(in_line & (p > z))
        def _():
            z_copy(at, 0, above).start()

        @pl.when(in_line & (p < z))
        def _():
            z_copy(at, 1, below).start()

        @pl.when(cross & jnp.logical_not(special))
        def _():
            x_out[at] = total[slot].astype(bf16)
            x_copy(at).start()

        @pl.when(cross & special & (p > z))
        def _():
            e_out[0] = total[slot].astype(bf16)
            e_copy(0, above).start()

        @pl.when(cross & special & (p < z))
        def _():
            e_out[1] = total[slot].astype(bf16)
            e_copy(1, below).start()

    def sent(ref, count, sem):
        ref = ref.at[pl.ds(0, count)]
        pltpu.make_async_copy(ref, ref, sem).wait()

    def drain_gather():
        pieces, rows = gathered.at[:, :, my_cols], stats.at[:, c]
        sent(pieces, STEPS, g_core)
        sent(rows, Z * X, s_core)
        sent(rows, Z, s_x)

        @pl.when(end)
        def _():
            sent(pieces, 7, g_x)
            sent(pieces, 3, g_z)
            sent(rows, 1, s_z)

        @pl.when(mid)
        def _():
            sent(pieces, 6, g_x)
            sent(pieces, 12, g_z)
            sent(rows, 5, s_z)

    def down_dot(slot):
        pltpu.make_async_copy(dw_buf.at[slot], dw_buf.at[slot], dw_sem.at[slot]).wait()
        return jnp.dot(hidden[...], dw_buf[slot], preferred_element_type=f32)

    def reduce_step(i, carry):
        @pl.when(i < STEPS)
        def _():
            part = down_dot(lax.rem(i, SLOTS))
            core_out[i] = part[:, :half].astype(bf16)
            core_copy(i).start()
            total[lax.rem(i, 2)] = part[:, half:]

        @pl.when(i < STEPS - SLOTS)
        def _():
            for copy in down(i + SLOTS):
                copy.start()

        @pl.when(i > 2)
        def _():
            with jax.named_scope("finish"):
                finish(i - 1)

        @pl.when(i == STEPS - 2)
        def _():
            drain_gather()

        return carry

    pltpu.make_async_copy(
        w_buf.at[(STEPS - 1) % SLOTS], w_buf.at[(STEPS - 1) % SLOTS], w_sem.at[(STEPS - 1) % SLOTS]
    ).wait()
    arrived(STEPS - 1, 1 - c)
    with jax.named_scope("boundary"):
        lax.fori_loop(0, 2, boundary, 0)
    for i in range(2):
        for copy in down(i + SLOTS):
            copy.start()
    with jax.named_scope("reduce"):
        lax.fori_loop(2, STEPS + 1, reduce_step, 0)

    sent(core_out, STEPS, core_send)
    sent(z_out, (Z - 1) * H, z_send)

    @pl.when(end)
    def _():
        sent(x_out, 7, x_send)
        sent(e_out, 1, e_send)

    @pl.when(mid)
    def _():
        sent(x_out, 6, x_send)
        sent(e_out, 2, e_send)


def fused(activations, norm_gain, gate_weight, up_weight, down_weight):
    tokens, feat = activations.shape
    wide = gate_weight.shape[1]
    n, half = 2 * Z * X, feat // H
    bf16, f32 = jnp.bfloat16, jnp.float32
    anywhere = pl.BlockSpec(memory_space=pl.ANY)
    vmem = pl.BlockSpec(memory_space=pltpu.VMEM)
    dma = pltpu.SemaphoreType.DMA
    return pl.pallas_call(
        kernel,
        out_shape=pltpu.VMEM((tokens, feat), bf16),
        in_specs=[anywhere, vmem, anywhere, anywhere, anywhere],
        out_specs=vmem,
        scratch_shapes=[
            pltpu.VMEM((tokens, feat), bf16),
            pltpu.VMEM((STEPS, tokens, 2 * half), bf16),
            pltpu.VMEM((Z * X, 2, 8, 128), f32),
            pltpu.VMEM((tokens, 128), f32),
            pltpu.VMEM((tokens, 128), f32),
            pltpu.VMEM((SLOTS, 2, 2 * half, wide), bf16),
            pltpu.VMEM((2, tokens, wide), f32),
            pltpu.VMEM((tokens, wide), bf16),
            pltpu.VMEM((SLOTS, wide, 2 * half), bf16),
            pltpu.VMEM((STEPS, tokens, half), bf16),
            pltpu.VMEM((STEPS, tokens, half), bf16),
            pltpu.VMEM((Z * H, tokens, half), bf16),
            pltpu.VMEM((Z * H, tokens, half), bf16),
            pltpu.VMEM((Z * H, tokens, half), bf16),
            pltpu.VMEM((2, Z * H, tokens, half), bf16),
            pltpu.VMEM((2, tokens, half), bf16),
            pltpu.VMEM((2, tokens, half), bf16),
            pltpu.VMEM((2, tokens, half), f32),
            dma,
            dma((SLOTS,)),
            dma((SLOTS,)),
            dma((Z * X,)),
            dma,
            dma,
            dma,
            dma,
            dma((STEPS, 2)),
            dma,
            dma,
            dma,
            dma,
            dma((STEPS,)),
            dma,
            dma((Z * H,)),
            dma,
            dma((2, Z * H)),
            dma,
            dma((2,)),
            dma((2,)),
            dma((2,)),
        ],
        compiler_params=pltpu.CompilerParams(
            collective_id=0, has_side_effects=True, vmem_limit_bytes=62 * 2**20
        ),
    )(activations, norm_gain.reshape(feat // 128, 128), gate_weight, up_weight, down_weight)


def solution(mesh):
    in_specs = (P("groups", "row"), P("row"), P(None, "row"), P(None, "row"), P("row", None))
    out_specs = P("groups", "row")
    n = mesh.shape["row"]

    def per_device(activations, norm_gain, gate_weight, up_weight, down_weight):
        tokens, feat = activations.shape
        fits = (
            n == 2 * Z * X
            and tokens % 128 == 0
            and tokens // 128 <= 8
            and feat % (128 * H) == 0
            and gate_weight.shape[1] % COLS == 0
        )
        body = fused if fits else plain
        return body(activations, norm_gain, gate_weight, up_weight, down_weight)

    return jax.shard_map(
        per_device, mesh=mesh, in_specs=in_specs, out_specs=out_specs, check_vma=False
    )
```
